32 devices in a mesh: lat: 4 (over y, x), lon: 8 (over z, core).
Axes of the slice: x: 2, y: 2, z: 4, core: 2. Of those that a mesh axis runs over, the one named last changes fastest.
Arguments:
- atmos_patch_tokens: bfloat16 [64, 192, 512], P('lat', 'lon'), may hold values from -6 to 6
- atmos_norm_gain: float32 [512], replicated, may hold values from 0.5 to 1.5
- query_key_value_weight: bfloat16 [512, 1536], replicated, may hold values from -0.25 to 0.25
- query_key_value_bias: float32 [1536], replicated, may hold values from -3 to 3
- relative_bias_grid: float32 [16, 225], replicated, may hold values from -260 to 260
- attention_output_weight: bfloat16 [512, 512], replicated, may hold values from -0.25 to 0.25
- flux_projector: bfloat16 [512, 16], replicated, may hold values from -0.25 to 0.25
- surface_encoder: float32 [4, 512], replicated, may hold values from -1.5 to 1.5
- ocean_cell_state: bfloat16 [64, 256, 256], P('lat', 'lon'), may hold values from -6 to 6
- land_sea_mask: int32 [64, 256], P('lat', 'lon'), may hold values 0 or 1
- depthwise_conv_kernel: float32 [7, 7, 256], replicated, may hold values from -0.875 to 0.875
- depthwise_conv_bias: float32 [256], replicated, may hold values from -3 to 3
- ocean_norm_gain: float32 [256], replicated, may hold values from 0.5 to 1.5
- pointwise_expand: bfloat16 [256, 1024], replicated, may hold values from -0.375 to 0.375
- pointwise_contract: bfloat16 [1024, 256], replicated, may hold values from -0.1875 to 0.1875
- layer_update_scale: float32 [256], replicated, may hold values from 0.3 to 1.5
- forcing_encoder: float32 [16, 256], replicated, may hold values from -1.5 to 1.5
- surface_projector: float32 [256, 4], replicated, may hold values from -0.375 to 0.375
- overlay_area_weight: bfloat16 [4, 8, 3, 64, 512], P('lat', 'lon'), may hold values from 0 to 1, as said below
- owners: int32 [4, 8, 3], P('lat', 'lon'), may hold values from 0 to 7, as said below
- owner_tile_blocks: int32 [4, 8, 3], P('lat', 'lon'), may hold values from 0 to 5
- counts: int32 [4, 8], P('lat', 'lon'), may hold values from 1 to 3
Outputs:
- atm_out: bfloat16 [64, 192, 512], P('lat', 'lon')
- ocean_out: bfloat16 [64, 256, 256], P('lat', 'lon')
The draws below stay inside these ranges and needn't reach their ends.
Inputs may be any that keep to these rules, and one draw needn't show every extreme that they name: `overlay_area_weight`: nonnegative. `owners`: each slot's owner is the ocean tile's own longitude strip or one of the two beside it, cyclically. `owner_tile_blocks`: values of unused slots are arbitrary within the range.
All inputs are finite; a program needn't handle non-finite values. No bound on the sum of `land_sea_mask` on one device may be relied on, other than what follows from the above.
Results may differ from the reference program's by a relative error of at most 0.008.
Values may be sent and summed in bfloat16 or wider, within the bound.
No kernel may reach another device: no remote copies, remote signals or barrier semaphores. Data moves between devices by JAX's collectives and lax.ppermute only.
A program may use at most 64 MiB of HBM per device.

```python
import math
import jax
import jax.numpy as jnp
from jax import lax

ATMOS_WIDTH = 512
HEADS = 16
WIN = 8
SHIFT = 4
ATMOS_PATCH_ROWS = 16
ATMOS_PATCH_COLS = 24
BLK = 64
OCEAN_WIDTH = 256
HID = 1024
KER = 7
OH = 16
OW = 32
FLUX = 16
SURFACE_FIELDS = 4
SLOTS = 3
NLAT_P = 64
NLON_P = 192
NOLAT = 64
NOLON = 256
N_LAT = 4
N_LON = 8


def draw_relative_bias_grid(key, part):
    entries = (2 * WIN - 1) ** 2
    lookup = jnp.clip(jax.random.normal(key, (HEADS, entries), jnp.float32), -4.0, 4.0)
    return lookup


def draw_overlay_area_weight(key, part):
    cells = OH * OW
    shape = (N_LAT, N_LON, SLOTS, BLK, cells)
    links = (jax.random.randint(jax.random.fold_in(key, 21), shape, 0, cells) < 6).astype(jnp.float32)
    values = jax.random.uniform(jax.random.fold_in(key, 22), shape, jnp.float32, 0.25, 0.75)
    return (links * values).astype(jnp.bfloat16)


def draw_owners(key, part):
    offsets = jax.random.randint(jax.random.fold_in(key, 31), (N_LAT, N_LON, SLOTS), -1, 2)
    strips = jnp.arange(N_LON, dtype=jnp.int32)[None, :, None]
    return ((strips + offsets + N_LON) % N_LON).astype(jnp.int32)


def set_ends(result, stream_key, low, high):
    dims = result.shape
    index_at = [jax.random.randint(jax.random.fold_in(stream_key, axis), (), 0, dims[axis]) for axis in range(len(dims))]
    result = result.at[tuple(index_at)].set(low)
    longest = dims.index(max(dims))
    index_at[longest] = (index_at[longest] + 1) % dims[longest]
    return result.at[tuple(index_at)].set(high)


def shard_levels(own_key, extent, split, low, high):
    level = 1.0
    for axis_at, parts in split:
        heights = jax.random.uniform(jax.random.fold_in(jax.random.fold_in(own_key, 6), axis_at), (parts,), jnp.float32, low / len(split), high / len(split))
        level = level * jnp.repeat(jnp.exp(heights), extent[axis_at] // parts).reshape((-1,) + (1,) * (len(extent) - 1 - axis_at))
    return level


def scatter_about(key, shape, scale, limit, cuts=(), kind=jnp.bfloat16):
    gain = shard_levels(key, shape, cuts, -0.22, 0.18) if cuts else 1.0
    values = jax.random.normal(key, shape, jnp.float32) * scale * gain
    return jnp.minimum(jnp.maximum(values, -limit), limit).astype(kind)


def setup_inputs(seed: int = 0) -> dict:
    keys = jax.random.split(jax.random.key(seed), 23)
    return {
        "atmos_patch_tokens": scatter_about(keys[0], (NLAT_P, NLON_P, ATMOS_WIDTH), 1.0, 6.0, ((0, 4), (1, 8))),
        "atmos_norm_gain": jnp.clip(1.0 + 0.1 * jax.random.normal(keys[1], (ATMOS_WIDTH,), jnp.float32), 0.5, 1.5),
        "query_key_value_weight": scatter_about(keys[2], (ATMOS_WIDTH, 3 * ATMOS_WIDTH), ATMOS_WIDTH ** -0.5, 0.25),
        "query_key_value_bias": scatter_about(keys[3], (3 * ATMOS_WIDTH,), 0.5, 3.0, (), jnp.float32),
        "relative_bias_grid": draw_relative_bias_grid(jax.random.fold_in(keys[22], 71), 0),
        "attention_output_weight": scatter_about(keys[5], (ATMOS_WIDTH, ATMOS_WIDTH), ATMOS_WIDTH ** -0.5, 0.25),
        "flux_projector": scatter_about(keys[6], (ATMOS_WIDTH, FLUX), ATMOS_WIDTH ** -0.5, 0.25),
        "surface_encoder": scatter_about(keys[7], (SURFACE_FIELDS, ATMOS_WIDTH), (4 * SURFACE_FIELDS) ** -0.5, 1.5, (), jnp.float32),
        "ocean_cell_state": scatter_about(keys[8], (NOLAT, NOLON, OCEAN_WIDTH), 1.0, 6.0, ((0, 4), (1, 8))),
        "land_sea_mask": set_ends((jax.random.randint(keys[9], (NOLAT, NOLON), 0, 4) < 3).astype(jnp.int32), jax.random.fold_in(keys[9], 1), 0, 1),
        "depthwise_conv_kernel": scatter_about(keys[10], (KER, KER, OCEAN_WIDTH), (KER * KER) ** -0.5, 0.875, (), jnp.float32),
        "depthwise_conv_bias": scatter_about(keys[11], (OCEAN_WIDTH,), 0.5, 3.0, (), jnp.float32),
        "ocean_norm_gain": jnp.clip(1.0 + 0.1 * jax.random.normal(keys[12], (OCEAN_WIDTH,), jnp.float32), 0.5, 1.5),
        "pointwise_expand": scatter_about(keys[13], (OCEAN_WIDTH, HID), OCEAN_WIDTH ** -0.5, 0.375),
        "pointwise_contract": scatter_about(keys[14], (HID, OCEAN_WIDTH), HID ** -0.5, 0.1875),
        "layer_update_scale": jnp.clip(jnp.exp(jax.random.uniform(keys[15], (OCEAN_WIDTH,), jnp.float32, math.log(0.3), math.log(1.5))), 0.3, 1.5),
        "forcing_encoder": scatter_about(keys[16], (FLUX, OCEAN_WIDTH), FLUX ** -0.5, 1.5, (), jnp.float32),
        "surface_projector": scatter_about(keys[17], (OCEAN_WIDTH, SURFACE_FIELDS), OCEAN_WIDTH ** -0.5, 0.375, (), jnp.float32),
        "overlay_area_weight": draw_overlay_area_weight(jax.random.fold_in(keys[22], 71), 0),
        "owners": draw_owners(jax.random.fold_in(keys[22], 71), 0),
        "owner_tile_blocks": set_ends(jax.random.randint(keys[20], (N_LAT, N_LON, SLOTS), 0, ATMOS_PATCH_ROWS * ATMOS_PATCH_COLS // BLK), jax.random.fold_in(keys[20], 1), 0, (ATMOS_PATCH_ROWS * ATMOS_PATCH_COLS // BLK) - 1).astype(jnp.int32),
        "counts": set_ends(jax.random.randint(keys[21], (N_LAT, N_LON), 1, SLOTS + 1), jax.random.fold_in(keys[21], 1), 1, SLOTS).astype(jnp.int32),
    }


FULL_PRECISION = lax.Precision.HIGHEST

def layer_norm(values, gain_vector, epsilon):
    average = lax.optimization_barrier(jnp.mean(values, axis=-1, keepdims=True))
    centred = values - average
    spread = lax.optimization_barrier(jnp.mean(centred * centred, axis=-1, keepdims=True))
    return centred * lax.rsqrt(spread + epsilon) * gain_vector

def to_windows(values, window):
    row_count, col_count, channel_total = values.shape
    pieces = values.reshape(row_count // window, window, col_count // window, window, channel_total).transpose(0, 2, 1, 3, 4)
    return pieces.reshape(-1, window * window, channel_total)

def from_windows(values, row_count, col_count, window):
    channel_total = values.shape[-1]
    pieces = values.reshape(row_count // window, col_count // window, window, window, channel_total).transpose(0, 2, 1, 3, 4)
    return pieces.reshape(row_count, col_count, channel_total)

def position_bias(lookup, window):
    places = jnp.arange(window * window, dtype=jnp.int32)
    row_place = places // window
    col_place = places % window
    offsets = (row_place[:, None] - row_place[None, :] + window - 1) * (2 * window - 1) + (col_place[:, None] - col_place[None, :] + window - 1)
    onehot = (offsets[:, :, None] == jnp.arange((2 * window - 1) ** 2, dtype=jnp.int32)[None, None, :]).astype(jnp.float32)
    return jnp.einsum('hp,abp->hab', lookup, onehot, precision=FULL_PRECISION)

def window_attention(normed, region, query_key_value_weight, query_key_value_bias, pos_bias, attention_output_weight, head_count, window):
    row_count, col_count, feature_width = normed.shape
    head_size = feature_width // head_count
    qkv = jnp.dot(normed.reshape(row_count * col_count, feature_width), query_key_value_weight, preferred_element_type=jnp.float32) + query_key_value_bias
    queries = (qkv[:, :feature_width] * head_size ** (-0.5)).astype(jnp.bfloat16)
    key_rows = qkv[:, feature_width:2 * feature_width].astype(jnp.bfloat16)
    value_rows = qkv[:, 2 * feature_width:].astype(jnp.bfloat16)

    def split_heads(matrix):
        return to_windows(matrix.reshape(row_count, col_count, feature_width), window).reshape(-1, window * window, head_count, head_size)
    queries = split_heads(queries)
    key_rows = split_heads(key_rows)
    value_rows = split_heads(value_rows)
    labels = to_windows(region.reshape(row_count, col_count, 1), window)[:, :, 0]
    scores = jnp.einsum('wahd,wbhd->whab', queries.astype(jnp.float32), key_rows.astype(jnp.float32)) + pos_bias[None]
    same_region = labels[:, None, :, None] == labels[:, None, None, :]
    scores = jnp.where(same_region, scores, -1000000000.0)
    largest = lax.optimization_barrier(jnp.max(scores, axis=-1, keepdims=True))
    expo = jnp.exp(scores - largest)
    weights = (expo / lax.optimization_barrier(jnp.sum(expo, axis=-1, keepdims=True))).astype(jnp.bfloat16)
    attended = jnp.einsum('whab,wbhd->wahd', weights.astype(jnp.float32), value_rows.astype(jnp.float32)).astype(jnp.bfloat16)
    attended = from_windows(attended.reshape(-1, window * window, feature_width), row_count, col_count, window)
    attended = attended.reshape(row_count * col_count, feature_width)
    projected = jnp.dot(attended, attention_output_weight, preferred_element_type=jnp.float32).astype(jnp.bfloat16)
    return projected.reshape(row_count, col_count, feature_width)

def reference(atmos_patch_tokens, atmos_norm_gain, query_key_value_weight, query_key_value_bias, relative_bias_grid, attention_output_weight, flux_projector, surface_encoder, ocean_cell_state, land_sea_mask, depthwise_conv_kernel, depthwise_conv_bias, ocean_norm_gain, pointwise_expand, pointwise_contract, layer_update_scale, forcing_encoder, surface_projector, overlay_area_weight, owners, owner_tile_blocks, counts):
    latitude_count = N_LAT
    longitude_count = N_LON
    ocean_cell_grid = OH * OW
    block_count = ATMOS_PATCH_ROWS * ATMOS_PATCH_COLS // BLK
    latitude_rows = ATMOS_PATCH_ROWS * latitude_count
    longitude_columns = ATMOS_PATCH_COLS * longitude_count
    ocean_rows = OH * latitude_count
    ocean_cols = OW * longitude_count
    wet_cell_mask = land_sea_mask.astype(jnp.float32)
    in_use = (jnp.arange(SLOTS, dtype=jnp.int32)[None, None, :] < counts[:, :, None]).astype(jnp.float32)
    owner_hot = (owners[..., None] == jnp.arange(longitude_count, dtype=jnp.int32)).astype(jnp.float32) * in_use[..., None]
    block_hot = (owner_tile_blocks[..., None] == jnp.arange(block_count, dtype=jnp.int32)).astype(jnp.float32)
    ocean_mask_float = ocean_cell_state.astype(jnp.float32)
    surface_values = jnp.einsum('jev,vh->jeh', ocean_mask_float, surface_projector, precision=FULL_PRECISION) * wet_cell_mask[:, :, None]
    surface_values = surface_values.astype(jnp.bfloat16)
    surface_tiles = surface_values.reshape(latitude_count, OH, longitude_count, OW, SURFACE_FIELDS).transpose(0, 2, 1, 3, 4).reshape(latitude_count, longitude_count, ocean_cell_grid, SURFACE_FIELDS)
    regrid_float = overlay_area_weight.astype(jnp.float32)
    contrib = jnp.einsum('ijktc,ijcs->ijkts', regrid_float, surface_tiles.astype(jnp.float32), precision=FULL_PRECISION)
    toward_atmosphere = jnp.einsum('ijkm,ijkb,ijkts->imbts', owner_hot, block_hot, contrib, precision=FULL_PRECISION)
    sea_surface_atmos = toward_atmosphere.reshape(latitude_count, longitude_count, ATMOS_PATCH_ROWS, ATMOS_PATCH_COLS, SURFACE_FIELDS).transpose(0, 2, 1, 3, 4).reshape(latitude_rows, longitude_columns, SURFACE_FIELDS)
    spatial_mixed = (atmos_patch_tokens.astype(jnp.float32) + jnp.einsum('fnw,wl->fnl', sea_surface_atmos, surface_encoder, precision=FULL_PRECISION)).astype(jnp.bfloat16)
    normed = layer_norm(spatial_mixed.astype(jnp.float32), atmos_norm_gain, 1e-05).astype(jnp.bfloat16)
    rolled = jnp.roll(normed, (-SHIFT, -SHIFT), (0, 1))
    region = (jnp.arange(latitude_rows, dtype=jnp.int32) >= latitude_rows - SHIFT).astype(jnp.int32)
    region = jnp.broadcast_to(region[:, None], (latitude_rows, longitude_columns))
    pos_bias = position_bias(relative_bias_grid, WIN)
    band_count = latitude_rows // WIN

    def one_band(pieces):
        return window_attention(pieces[0], pieces[1], query_key_value_weight, query_key_value_bias, pos_bias, attention_output_weight, HEADS, WIN)
    projected = lax.map(one_band, (rolled.reshape(band_count, WIN, longitude_columns, ATMOS_WIDTH), region.reshape(band_count, WIN, longitude_columns)))
    projected = projected.reshape(latitude_rows, longitude_columns, ATMOS_WIDTH)
    back = jnp.roll(projected, (SHIFT, SHIFT), (0, 1))
    atm_out = (spatial_mixed.astype(jnp.float32) + back.astype(jnp.float32)).astype(jnp.bfloat16)
    flux = jnp.dot(atm_out.reshape(latitude_rows * longitude_columns, ATMOS_WIDTH), flux_projector, preferred_element_type=jnp.float32).astype(jnp.bfloat16)
    flux_tiles = flux.reshape(latitude_count, ATMOS_PATCH_ROWS, longitude_count, ATMOS_PATCH_COLS, FLUX).transpose(0, 2, 1, 3, 4).reshape(latitude_count, longitude_count, block_count, BLK, FLUX)
    picked = jnp.einsum('ijkm,ijkb,imbtf->ijktf', owner_hot, block_hot, flux_tiles.astype(jnp.float32), precision=FULL_PRECISION)
    forcing = jnp.einsum('ijktc,ijktf->ijcf', regrid_float, picked, precision=FULL_PRECISION)
    forcing = forcing.reshape(latitude_count, longitude_count, OH, OW, FLUX).transpose(0, 2, 1, 3, 4).reshape(ocean_rows, ocean_cols, FLUX)
    half = KER // 2
    padded = jnp.pad(ocean_mask_float, ((half, half), (0, 0), (0, 0)))
    padded = jnp.concatenate([padded[:, ocean_cols - half:], padded, padded[:, :half]], axis=1)
    conv = jnp.zeros_like(ocean_mask_float) + depthwise_conv_bias
    for row_off in range(KER):
        for col_off in range(KER):
            conv = conv + depthwise_conv_kernel[row_off, col_off] * padded[row_off:row_off + ocean_rows, col_off:col_off + ocean_cols]
    pre = conv + jnp.einsum('rcf,fx->rcx', forcing, forcing_encoder, precision=FULL_PRECISION)

    def pointwise(pieces):
        pre_band, state_band, mask_band = pieces
        ocean_normed = layer_norm(pre_band, ocean_norm_gain, 1e-06).astype(jnp.bfloat16)
        hidden = jax.nn.gelu(jnp.dot(ocean_normed, pointwise_expand, preferred_element_type=jnp.float32), approximate=False).astype(jnp.bfloat16)
        update = jnp.dot(hidden, pointwise_contract, preferred_element_type=jnp.float32)
        return (state_band + mask_band[:, None] * layer_update_scale * update).astype(jnp.bfloat16)
    band_cells = OH * ocean_cols
    ocean_out = lax.map(pointwise, (pre.reshape(latitude_count, band_cells, OCEAN_WIDTH), ocean_mask_float.reshape(latitude_count, band_cells, OCEAN_WIDTH), wet_cell_mask.reshape(latitude_count, band_cells)))
    ocean_out = ocean_out.reshape(ocean_rows, ocean_cols, OCEAN_WIDTH)
    return (atm_out, ocean_out)
```

```python
import functools

import jax
import jax.numpy as jnp
from jax import lax
from jax.experimental import pallas as pl
from jax.experimental.pallas import tpu as pltpu
from jax.sharding import PartitionSpec as P

HEADS = 16
WIN = 8
SHIFT = 4
BLK = 64
KER = 7
HALF = KER // 2
F32 = jnp.float32
BF16 = jnp.bfloat16
VMEM_LIMIT = 48 * 1024 * 1024


def dot(a, b, dims=((1,), (0,))):
    return lax.dot_general(a, b, (dims, ((), ())), preferred_element_type=F32)


def iota(shape, dim):
    return lax.broadcasted_iota(jnp.int32, shape, dim)


def split2(x):
    high = x.astype(BF16)
    return high.astype(F32), (x - high.astype(F32)).astype(BF16).astype(F32)


def split3(x):
    high, rest = x.astype(BF16), x
    rest = rest - high.astype(F32)
    middle = rest.astype(BF16)
    return high.astype(F32), middle.astype(F32), rest - middle.astype(F32)


def vmem():
    return pl.BlockSpec(memory_space=pltpu.VMEM)


def smem():
    return pl.BlockSpec(memory_space=pltpu.SMEM)


def call(body, outs, args, scalars=0, scratch=(), flops=1e6, name=None):
    moved = sum(a.size * a.dtype.itemsize for a in args) + sum(
        o.size * o.dtype.itemsize for o in outs
    )
    result = pl.pallas_call(
        body,
        out_shape=tuple(outs),
        in_specs=[smem()] * scalars + [vmem()] * (len(args) - scalars),
        out_specs=tuple(vmem() for _ in outs),
        scratch_shapes=list(scratch),
        compiler_params=pltpu.CompilerParams(vmem_limit_bytes=VMEM_LIMIT),
        cost_estimate=pl.CostEstimate(
            flops=int(flops), bytes_accessed=int(moved), transcendentals=0
        ),
        name=name,
    )(*args)
    return result


def struct(shape, dtype):
    return jax.ShapeDtypeStruct(shape, dtype)


def pack_lat_body(tok, sea, to_a, to_b):
    even = lax.rem(lax.axis_index("lat"), 2) == 0
    rows, cols, width = tok.shape
    sea_rows, sea_cols, _ = sea.shape

    def put(dst, bottom):
        start = jnp.where(bottom, rows - SHIFT, 0)
        dst[:, :cols, :width] = tok[pl.ds(start, SHIFT)]
        start = jnp.where(bottom, sea_rows - HALF, 0)
        dst[:HALF, :sea_cols, width:] = sea[pl.ds(start, HALF)]

    put(to_a, even)
    put(to_b, jnp.logical_not(even))


def pack_lon_body(tok, sea, from_a, from_b, to_core, to_chip):
    lat_even = lax.rem(lax.axis_index("lat"), 2) == 0
    lon_even = lax.rem(lax.axis_index("lon"), 2) == 0
    rows, cols, width = tok.shape
    sea_rows, sea_cols, _ = sea.shape

    def put(at, sea_at, token_rows, sea_part):
        token_rows = token_rows.astype(F32)
        sea_part = sea_part.astype(F32)
        first, last = token_rows[:, :SHIFT], token_rows[:, cols - SHIFT :]
        count = token_rows.shape[0]
        to_core[at : at + count, :, :width] = jnp.where(lon_even, last, first).astype(BF16)
        to_chip[at : at + count, :, :width] = jnp.where(lon_even, first, last).astype(BF16)
        first, last = sea_part[:, :HALF], sea_part[:, sea_cols - HALF :]
        count = sea_part.shape[0]
        to_core[sea_at : sea_at + count, :HALF, width:] = jnp.where(
            lon_even, last, first
        ).astype(BF16)
        to_chip[sea_at : sea_at + count, :HALF, width:] = jnp.where(
            lon_even, first, last
        ).astype(BF16)

    put(SHIFT, HALF, tok[...], sea[...])

    def halos(north, south):
        put(0, 0, north[:, :cols, :width], north[:HALF, :sea_cols, width:])
        put(
            rows + SHIFT,
            sea_rows + HALF,
            south[:, :cols, :width],
            south[:HALF, :sea_cols, width:],
        )

    @pl.when(lat_even)
    def _():
        halos(from_b, from_a)

    @pl.when(jnp.logical_not(lat_even))
    def _():
        halos(from_a, from_b)


def slot_base(owners, blocks, counts, k, block_count):
    lon = lax.axis_index("lon")
    size = lax.axis_size("lon")
    relative = lax.rem(owners[0, 0, k] - lon + 1 + size, size)
    base = (relative * block_count + blocks[0, 0, k]) * BLK
    return jnp.where(k < counts[0, 0], base, -(1 << 20))


def slot_targets(owners, blocks, counts, places, slot_count, block_count):
    slot = places // BLK
    target = places - slot * BLK
    for k in range(slot_count):
        base = slot_base(owners, blocks, counts, k, block_count)
        target = target + jnp.where(slot == k, base, 0)
    return target


def mask_row(mask):
    rows, cols = mask.shape
    cells = rows * cols
    spread = (iota((cols, cells), 1) % cols == iota((cols, cells), 0)).astype(BF16)
    wide = dot(mask.astype(F32).astype(BF16), spread)
    own = iota((rows, cells), 1) // cols == iota((rows, cells), 0)
    return jnp.sum(jnp.where(own, wide, 0.0), axis=0, keepdims=True)


def mask_column(mask):
    rows, cols = mask.shape
    cells = rows * cols
    spread = (iota((cells, rows), 0) // cols == iota((cells, rows), 1)).astype(BF16)
    wide = dot(spread, mask.astype(F32).astype(BF16))
    own = iota((cells, cols), 0) % cols == iota((cells, cols), 1)
    return jnp.sum(jnp.where(own, wide, 0.0), axis=1, keepdims=True)


def surface_body(
    block_count, owners, blocks, counts, sea, mask, projector, overlay, east, west, to_core, to_chip
):
    slot_count = overlay.shape[0] // BLK
    fields = projector.shape[0]
    patches = block_count * BLK
    cells = sea[...]
    parts = jnp.concatenate(split3(projector[...]), axis=0).astype(BF16)
    spread = dot(parts, cells, ((1,), (1,)))
    values = spread[:fields] + spread[fields : 2 * fields] + spread[2 * fields :]
    values = (values * mask_row(mask[...])).astype(BF16)
    contrib = dot(values, overlay[...], ((1,), (1,)))
    stacked = jnp.concatenate(split3(contrib), axis=0).astype(BF16)
    shape = (slot_count * BLK, 3 * patches)
    places = iota((shape[0], 1), 0)
    target = slot_targets(owners, blocks, counts, places, slot_count, block_count)
    route = (iota(shape, 1) == target).astype(F32).astype(BF16)
    routed = dot(stacked, route)
    routed = routed[:fields] + routed[fields : 2 * fields] + routed[2 * fields :]
    to_west = routed[:, :patches]
    own = routed[:, patches : 2 * patches]
    to_east = routed[:, 2 * patches :]
    east_pack = jnp.concatenate([to_east, own], axis=0)
    west_pack = jnp.concatenate([to_west, own], axis=0)
    even = lax.rem(lax.axis_index("lon"), 2) == 0
    east[...] = east_pack
    west[...] = west_pack
    to_core[...] = jnp.where(even, east_pack, west_pack)
    to_chip[...] = jnp.where(even, west_pack, east_pack)


def gather_body(east, west, from_core, from_chip, from_far_west, from_far_east, out):
    fields = out.shape[0] // 4
    even = lax.rem(lax.axis_index("lon"), 2) == 0
    core, chip = from_core[...], from_chip[...]
    from_west = jnp.where(even, chip, core)
    from_east = jnp.where(even, core, chip)
    own_east, own_west = east[...], west[...]
    own = own_east[fields:] + from_west[:fields] + from_east[:fields]
    beside_west = from_far_west[...][:fields] + from_west[fields:] + own_west[:fields]
    beside_east = own_east[:fields] + from_east[fields:] + from_far_east[...][:fields]
    out[...] = jnp.concatenate([own, beside_west, beside_east, jnp.zeros_like(own)], axis=0)


def attention_body(
    tok,
    from_a,
    from_b,
    from_core,
    from_chip,
    sst,
    sst_a,
    sst_b,
    gain,
    weight,
    weight_bias,
    pos_bias,
    out_weight,
    projector,
    encoder,
    atm,
    flux,
    grid,
    fields_grid,
    head_mask,
):
    rows, cols, width = tok.shape
    padded_rows, padded_cols = rows + 2 * SHIFT, cols + 2 * SHIFT
    band_count, per_band = padded_rows // WIN, padded_cols // WIN
    lat, lat_size = lax.axis_index("lat"), lax.axis_size("lat")
    lat_even = lax.rem(lat, 2) == 0
    lon_even = lax.rem(lax.axis_index("lon"), 2) == 0
    head = width // HEADS
    group = 256 // head
    places = WIN * WIN
    inner = slice(SHIFT, SHIFT + cols)

    head_mask[...] = (
        (iota(head_mask.shape, 0) // places == iota(head_mask.shape, 1) // head)
        .astype(F32)
        .astype(BF16)
    )

    def fields_of(ref, lo, hi):
        values = ref[:, lo * cols : hi * cols]
        high, low = split2(values)
        turned = jnp.transpose(jnp.concatenate([high, low, high], axis=0))
        return turned.reshape(hi - lo, cols, turned.shape[1])

    def put_fields(at, values):
        count = values.shape[0]
        span = values.shape[2]
        kind = (iota((1, 1, span), 2) % 16) // 4
        fields_grid[at : at + count, inner, :span] = jnp.where(kind == 0, values, 0.0)
        fields_grid[at : at + count, :SHIFT, :span] = jnp.where(
            kind == 1, values[:, cols - SHIFT :], 0.0
        )
        fields_grid[at : at + count, SHIFT + cols :, :span] = jnp.where(
            kind == 2, values[:, :SHIFT], 0.0
        )

    grid[SHIFT : SHIFT + rows, inner] = tok[...].astype(F32)
    put_fields(SHIFT, fields_of(sst, 0, rows))

    def lat_halos(north, south, sst_north, sst_south):
        grid[:SHIFT, inner] = north[:, :cols, :width].astype(F32)
        grid[SHIFT + rows :, inner] = south[:, :cols, :width].astype(F32)
        put_fields(0, fields_of(sst_north, rows - SHIFT, rows))
        put_fields(SHIFT + rows, fields_of(sst_south, 0, SHIFT))

    def lon_halos(west, east):
        grid[:, :SHIFT] = west[:, :, :width].astype(F32)
        grid[:, SHIFT + cols :] = east[:, :, :width].astype(F32)

    @pl.when(lat_even)
    def _():
        lat_halos(from_b, from_a, sst_b, sst_a)

    @pl.when(jnp.logical_not(lat_even))
    def _():
        lat_halos(from_a, from_b, sst_a, sst_b)

    @pl.when(lon_even)
    def _():
        lon_halos(from_chip, from_core)

    @pl.when(jnp.logical_not(lon_even))
    def _():
        lon_halos(from_core, from_chip)

    enc = encoder[...]
    enc = jnp.concatenate([enc, enc, enc, jnp.zeros_like(enc)], axis=0)
    enc_high, enc_low = split2(enc)
    enc_stack = jnp.concatenate([enc_high, enc_high, enc_low], axis=0).astype(BF16)
    span = enc_stack.shape[0]
    lane = iota((places, HEADS * places), 1) % places
    crosses = (lane // (places // 2)) != (iota((places, HEADS * places), 0) // (places // 2))
    lane128 = iota((places, 2 * places), 1)

    def band(b, carry):
        at = pl.multiple_of(b * WIN, WIN)
        state = jnp.concatenate(
            [
                grid[pl.ds(at, WIN), w * WIN : (w + 1) * WIN].reshape(places, width)
                for w in range(per_band)
            ],
            axis=0,
        )
        fields = jnp.concatenate(
            [
                fields_grid[pl.ds(at, WIN), w * WIN : (w + 1) * WIN, :span].reshape(places, span)
                for w in range(per_band)
            ],
            axis=0,
        )
        mixed = (state + dot(fields.astype(BF16), enc_stack)).astype(BF16).astype(F32)
        average = jnp.mean(mixed, axis=-1, keepdims=True)
        centred = mixed - average
        spread = jnp.mean(centred * centred, axis=-1, keepdims=True)
        normed = (centred * lax.rsqrt(spread + 1e-05) * gain[...]).astype(BF16)
        qkv = dot(normed, weight[...]) + weight_bias[...]
        queries = (qkv[:, :width] * head ** (-0.5)).astype(BF16)
        keys = qkv[:, width : 2 * width].astype(BF16)
        values = qkv[:, 2 * width :].astype(BF16)
        first_band = jnp.logical_and(lat == 0, b == 0)
        last_band = jnp.logical_and(lat == lat_size - 1, b == band_count - 1)
        penalty = jnp.where(jnp.logical_or(first_band, last_band), -1000000000.0, 0.0)
        bias = pos_bias[...] + jnp.where(crosses, penalty, 0.0)
        mask = head_mask[...]
        attended = []
        for w in range(per_band):
            pieces = []
            for g in range(HEADS // group):
                lanes = slice(g * group * head, (g + 1) * group * head)
                part = slice(w * places, (w + 1) * places)
                q, k, v = queries[part, lanes], keys[part, lanes], values[part, lanes]
                k_wide = jnp.concatenate([k] * group, axis=0) * mask
                v_wide = jnp.concatenate([v] * group, axis=0) * mask
                scores = dot(q, k_wide, ((1,), (1,)))
                scores = scores + bias[:, g * group * places : (g + 1) * group * places]
                weights = []
                for pair in range(group // 2):
                    s = scores[:, pair * 2 * places : (pair + 1) * 2 * places]
                    low = jnp.max(jnp.where(lane128 < places, s, -3e38), axis=1, keepdims=True)
                    high = jnp.max(jnp.where(lane128 < places, -3e38, s), axis=1, keepdims=True)
                    weights.append(jnp.exp(s - jnp.where(lane128 < places, low, high)))
                expo = jnp.concatenate(weights, axis=1).astype(BF16)
                total = dot(expo, mask)
                pieces.append((dot(expo, v_wide) / total).astype(BF16))
            attended.append(jnp.concatenate(pieces, axis=1))
        attended = jnp.concatenate(attended, axis=0)
        projected = dot(attended, out_weight[...]).astype(BF16).astype(F32)
        result = (mixed + projected).astype(BF16).astype(F32)
        for w in range(per_band):
            grid[pl.ds(at, WIN), w * WIN : (w + 1) * WIN] = result[
                w * places : (w + 1) * places
            ].reshape(WIN, WIN, width)
        return carry

    lax.fori_loop(0, band_count, band, 0)
    own = grid[SHIFT : SHIFT + rows, inner]
    atm[...] = own.astype(BF16)
    flat = own.reshape(rows * cols, width).astype(BF16)
    flux[...] = dot(projector[...], flat, ((1,), (1,))).astype(BF16)


def conv_body(sea, from_a, from_b, from_core, from_chip, kernel, bias, conv, grid):
    lat_even = lax.rem(lax.axis_index("lat"), 2) == 0
    lon_even = lax.rem(lax.axis_index("lon"), 2) == 0
    rows, cols, channels = sea.shape
    width = from_a.shape[2] - channels
    inner = slice(HALF, HALF + cols)
    grid[HALF : HALF + rows, inner] = sea[...].astype(F32)

    def lat_halos(north, south):
        grid[:HALF, inner] = north[:HALF, :cols, width:].astype(F32)
        grid[HALF + rows :, inner] = south[:HALF, :cols, width:].astype(F32)

    def lon_halos(west, east):
        count = rows + 2 * HALF
        grid[:, :HALF] = west[:count, :HALF, width:].astype(F32)
        grid[:, HALF + cols : 2 * HALF + cols] = east[:count, :HALF, width:].astype(F32)

    @pl.when(lat_even)
    def _():
        lat_halos(from_b, from_a)

    @pl.when(jnp.logical_not(lat_even))
    def _():
        lat_halos(from_a, from_b)

    @pl.when(lon_even)
    def _():
        lon_halos(from_chip, from_core)

    @pl.when(jnp.logical_not(lon_even))
    def _():
        lon_halos(from_core, from_chip)

    for c in range(0, channels, 128):
        lanes = slice(c, c + 128)
        for s in range(0, cols, 8):
            total = jnp.broadcast_to(bias[:, lanes].reshape(1, 1, 128), (rows, 8, 128))
            for v in range(KER):
                column = grid[:, s + v : s + v + 8, lanes]
                for u in range(KER):
                    tap = kernel[u, v : v + 1, lanes].reshape(1, 1, 128)
                    total = total + tap * column[u : u + rows]
            conv[:, s : s + 8, lanes] = total


def ocean_body(
    block_count,
    owners,
    blocks,
    counts,
    conv,
    flux,
    from_core,
    from_chip,
    overlay,
    encoder,
    gain,
    expand,
    contract,
    sea,
    mask,
    scale,
    out,
):
    slot_count = overlay.shape[0] // BLK
    patches = block_count * BLK
    even = lax.rem(lax.axis_index("lon"), 2) == 0
    core, chip = from_core[...].astype(F32), from_chip[...].astype(F32)
    west = jnp.where(even, chip, core).astype(BF16)
    east = jnp.where(even, core, chip).astype(BF16)
    around = jnp.concatenate([west, flux[...], east], axis=1)
    shape = (3 * patches, slot_count * BLK)
    places = iota((1, shape[1]), 1)
    target = slot_targets(owners, blocks, counts, places, slot_count, block_count)
    route = (iota(shape, 0) == target).astype(F32).astype(BF16)
    picked = dot(around, route).astype(BF16)
    forcing = dot(picked, overlay[...])
    high, low = split2(forcing)
    turned = jnp.transpose(jnp.concatenate([high, low, high], axis=0)).astype(BF16)
    enc_high, enc_low = split2(encoder[...])
    enc_stack = jnp.concatenate([enc_high, enc_high, enc_low], axis=0).astype(BF16)
    wet = mask_column(mask[...])
    cells = out.shape[0]
    chunk = cells // 2
    for at in range(0, cells, chunk):
        part = slice(at, at + chunk)
        pre = conv[part] + dot(turned[part], enc_stack)
        average = jnp.mean(pre, axis=-1, keepdims=True)
        centred = pre - average
        spread = jnp.mean(centred * centred, axis=-1, keepdims=True)
        normed = (centred * lax.rsqrt(spread + 1e-06) * gain[...]).astype(BF16)
        hidden = dot(normed, expand[...])
        hidden = (0.5 * hidden * (1.0 + lax.erf(hidden * 0.5**0.5))).astype(BF16)
        update = dot(hidden, contract[...])
        out[part] = (sea[part].astype(F32) + wet[part] * scale[...] * update).astype(BF16)


def position_bias(lookup):
    places = jnp.arange(WIN * WIN, dtype=jnp.int32)
    row_place, col_place = places // WIN, places % WIN
    span = 2 * WIN - 1
    offsets = (row_place[:, None] - row_place[None, :] + WIN - 1) * span + (
        col_place[:, None] - col_place[None, :] + WIN - 1
    )
    onehot = (offsets[:, :, None] == jnp.arange(span**2, dtype=jnp.int32)).astype(F32)
    wide = jnp.einsum("hp,abp->ahb", lookup, onehot, precision=lax.Precision.HIGHEST)
    return wide.reshape(WIN * WIN, -1)


def local(
    atmos_patch_tokens,
    atmos_norm_gain,
    query_key_value_weight,
    query_key_value_bias,
    relative_bias_grid,
    attention_output_weight,
    flux_projector,
    surface_encoder,
    ocean_cell_state,
    land_sea_mask,
    depthwise_conv_kernel,
    depthwise_conv_bias,
    ocean_norm_gain,
    pointwise_expand,
    pointwise_contract,
    layer_update_scale,
    forcing_encoder,
    surface_projector,
    overlay_area_weight,
    owners,
    owner_tile_blocks,
    counts,
):
    lat_size, lon_size = lax.axis_size("lat"), lax.axis_size("lon")
    rows, cols, width = atmos_patch_tokens.shape
    sea_rows, sea_cols, channels = ocean_cell_state.shape
    cells = sea_rows * sea_cols
    patches = rows * cols
    block_count = patches // BLK
    slot_count = owners.shape[2]
    channel_count = flux_projector.shape[1]

    def swaps(pairs):
        return [(a, b) for a, b in pairs] + [(b, a) for a, b in pairs]

    lat_a = swaps([(k, k + 1) for k in range(0, lat_size - 1, 2)])
    lat_b = swaps([(k, k + 1) for k in range(1, lat_size - 1, 2)])
    core = swaps([(k, k + 1) for k in range(0, lon_size, 2)])
    chip = swaps([(k + 1, (k + 2) % lon_size) for k in range(0, lon_size, 2)])
    two_east = [(k, (k + 2) % lon_size) for k in range(lon_size)]
    two_west = [(k, (k - 2) % lon_size) for k in range(lon_size)]

    tok, sea = atmos_patch_tokens, ocean_cell_state
    overlay = overlay_area_weight.reshape(slot_count * BLK, cells)
    lat_pack = struct((SHIFT, max(cols, sea_cols), width + channels), BF16)
    to_a, to_b = call(pack_lat_body, (lat_pack, lat_pack), (tok, sea), name="pack_lat")
    from_a = lax.ppermute(to_a, "lat", lat_a)
    from_b = lax.ppermute(to_b, "lat", lat_b)

    pack = struct((2 * surface_projector.shape[1], patches), F32)
    east, west, to_core, to_chip = call(
        functools.partial(surface_body, block_count),
        (pack,) * 4,
        (
            owners,
            owner_tile_blocks,
            counts,
            sea.reshape(cells, channels),
            land_sea_mask,
            surface_projector.T,
            overlay,
        ),
        scalars=3,
        flops=3e8,
        name="surface",
    )
    core_in = lax.ppermute(to_core, "lon", core)
    chip_in = lax.ppermute(to_chip, "lon", chip)
    far_west = lax.ppermute(east, "lon", two_east)
    far_east = lax.ppermute(west, "lon", two_west)

    lon_pack = struct((rows + 2 * SHIFT, SHIFT, width + channels), BF16)
    to_core, to_chip = call(
        pack_lon_body, (lon_pack, lon_pack), (tok, sea, from_a, from_b), name="pack_lon"
    )
    from_core = lax.ppermute(to_core, "lon", core)
    from_chip = lax.ppermute(to_chip, "lon", chip)

    (sst,) = call(
        gather_body,
        (struct((4 * surface_projector.shape[1], patches), F32),),
        (east, west, core_in, chip_in, far_west, far_east),
        name="gather",
    )
    sst_a = lax.ppermute(sst, "lat", lat_a)
    sst_b = lax.ppermute(sst, "lat", lat_b)

    pos_bias = position_bias(relative_bias_grid)
    padded = (rows + 2 * SHIFT, cols + 2 * SHIFT)
    atm, flux = call(
        attention_body,
        (struct((rows, cols, width), BF16), struct((channel_count, patches), BF16)),
        (
            tok,
            from_a,
            from_b,
            from_core,
            from_chip,
            sst,
            sst_a,
            sst_b,
            atmos_norm_gain.reshape(1, width),
            query_key_value_weight,
            query_key_value_bias.reshape(1, 3 * width),
            pos_bias,
            attention_output_weight,
            flux_projector.T,
            surface_encoder,
        ),
        scratch=(
            pltpu.VMEM((*padded, width), F32),
            pltpu.VMEM((*padded, 128), F32),
            pltpu.VMEM((512, 256), BF16),
        ),
        flops=3e9,
        name="attention",
    )
    flux_core = lax.ppermute(flux, "lon", core)
    flux_chip = lax.ppermute(flux, "lon", chip)

    (conv,) = call(
        conv_body,
        (struct((sea_rows, sea_cols, channels), F32),),
        (
            sea,
            from_a,
            from_b,
            from_core,
            from_chip,
            depthwise_conv_kernel,
            depthwise_conv_bias.reshape(1, channels),
        ),
        scratch=(pltpu.VMEM((sea_rows + 2 * HALF, sea_cols + 8, channels), F32),),
        flops=2e9,
        name="conv",
    )
    (ocean,) = call(
        functools.partial(ocean_body, block_count),
        (struct((cells, channels), BF16),),
        (
            owners,
            owner_tile_blocks,
            counts,
            conv.reshape(cells, channels),
            flux,
            flux_core,
            flux_chip,
            overlay,
            forcing_encoder,
            ocean_norm_gain.reshape(1, channels),
            pointwise_expand,
            pointwise_contract,
            sea.reshape(cells, channels),
            land_sea_mask,
            layer_update_scale.reshape(1, channels),
        ),
        scalars=3,
        flops=1e9,
        name="ocean",
    )
    return (atm, ocean.reshape(sea_rows, sea_cols, channels))


def solution(mesh):
    grid = P("lat", "lon", None)
    placed = (
        (grid,)
        + (P(),) * 7
        + (grid, P("lat", "lon"))
        + (P(),) * 8
        + (P("lat", "lon", None, None, None), grid, grid, P("lat", "lon"))
    )
    return jax.shard_map(
        local,
        mesh=mesh,
        in_specs=placed,
        out_specs=(grid, grid),
        check_vma=False,
    )
```

```python
import functools

import jax
import jax.numpy as jnp
from jax import lax
from jax.experimental import pallas as pl
from jax.experimental.pallas import tpu as pltpu
from jax.sharding import PartitionSpec as P


HEADS = 16
WIN = 8
SHIFT = 4
BLK = 64
KER = 7
HALF = KER // 2
F32 = jnp.float32
BF16 = jnp.bfloat16
VMEM_LIMIT = 48 * 1024 * 1024


def dot(a, b, dims=((1,), (0,))):
    return lax.dot_general(a, b, (dims, ((), ())), preferred_element_type=F32)


def iota(shape, dim):
    return lax.broadcasted_iota(jnp.int32, shape, dim)


def split2(x):
    high = x.astype(BF16)
    return high.astype(F32), (x - high.astype(F32)).astype(BF16).astype(F32)


def split3(x):
    high, rest = x.astype(BF16), x
    rest = rest - high.astype(F32)
    middle = rest.astype(BF16)
    return high.astype(F32), middle.astype(F32), rest - middle.astype(F32)


def pick(first_if, a, b):
    kind = a.dtype
    a, b = a.astype(F32), b.astype(F32)
    return (
        jnp.where(first_if, a, b).astype(kind),
        jnp.where(first_if, b, a).astype(kind),
    )


def vmem():
    return pl.BlockSpec(memory_space=pltpu.VMEM)


def smem():
    return pl.BlockSpec(memory_space=pltpu.SMEM)


def anywhere():
    return pl.BlockSpec(memory_space=pltpu.HBM)


def call(body, outs, args, specs=None, out_specs=None, scratch=(), flops=1e6):
    moved = sum(a.size * a.dtype.itemsize for a in args)
    return pl.pallas_call(
        body,
        out_shape=tuple(outs),
        in_specs=list(specs or [vmem()] * len(args)),
        out_specs=tuple(out_specs or [vmem()] * len(outs)),
        scratch_shapes=list(scratch),
        compiler_params=pltpu.CompilerParams(vmem_limit_bytes=VMEM_LIMIT),
        cost_estimate=pl.CostEstimate(
            flops=int(flops), bytes_accessed=int(moved), transcendentals=0
        ),
    )(*args)


def struct(shape, dtype):
    return jax.ShapeDtypeStruct(shape, dtype)


def lat_halos_of(lat_even, lat_a, lat_b, rows_cols, width, sea_cols):
    rows, cols = rows_cols
    count = rows * cols
    north, south = pick(lat_even, lat_b[:count], lat_a[:count])
    shape = (HALF, sea_cols, north.shape[1] - width)
    return (
        north[:, :width].reshape(rows, cols, width),
        south[:, :width].reshape(rows, cols, width),
        north[:, width:].reshape(shape),
        south[:, width:].reshape(shape),
    )


def put_columns(to_core, to_chip, at, values, count, lanes):
    lon_even = lax.rem(lax.axis_index("lon"), 2) == 0
    values = values.astype(F32)
    high, cols, _ = values.shape
    first, last = values[:, :count], values[:, cols - count :]
    to_core[at : at + high, :count, lanes] = jnp.where(lon_even, last, first).astype(BF16)
    to_chip[at : at + high, :count, lanes] = jnp.where(lon_even, first, last).astype(BF16)


def pack_body(
    cols, width, sea_cols, lat_a, lat_b, given, to_core, to_chip, far_one, far_two, sides
):
    fields = given.shape[0] // 3
    patches = given.shape[1]
    count = SHIFT * cols
    channels = lat_a.shape[1] - width
    lat_even = lax.rem(lax.axis_index("lat"), 2) == 0
    lon = lax.axis_index("lon")
    lon_even = lax.rem(lon, 2) == 0
    north, south, sea_north, sea_south = lat_halos_of(
        lat_even, lat_a, lat_b, (SHIFT, cols), width, sea_cols
    )
    lanes = slice(0, width)
    put_columns(to_core, to_chip, 0, north, SHIFT, lanes)
    put_columns(to_core, to_chip, SHIFT, south, SHIFT, lanes)
    lanes = slice(width, width + channels)
    put_columns(to_core, to_chip, 0, sea_north, HALF, lanes)
    put_columns(to_core, to_chip, SHIFT, sea_south, HALF, lanes)

    def pieces(ref):
        block = ref[count : count + 8].astype(F32)[:fields]
        return [
            block[:, 128 * k : 128 * k + 128] + block[:, 128 * (k + 3) : 128 * (k + 4)]
            for k in range(3)
        ]

    from_a, from_b = pieces(lat_a), pieces(lat_b)
    whole = []
    for k in range(3):
        whole.append(
            jnp.concatenate(
                [
                    jnp.where(lat_even, from_b[k], from_a[k]),
                    given[k * fields : (k + 1) * fields],
                    jnp.where(lat_even, from_a[k], from_b[k]),
                ],
                axis=1,
            )
        )
        sides[k * fields : (k + 1) * fields] = whole[k]
    to_west, own, to_east = [split2(w) for w in whole]
    span = patches + 256
    at = 2 * SHIFT
    for n in range(2):
        core_part = jnp.where(lon_even, to_east[n], to_west[n])
        chip_part = jnp.where(lon_even, to_west[n], to_east[n])
        to_core[at + 2 * n, :, :span] = core_part.astype(BF16)
        to_chip[at + 2 * n, :, :span] = chip_part.astype(BF16)
        to_core[at + 2 * n + 1, :, :span] = own[n].astype(BF16)
        to_chip[at + 2 * n + 1, :, :span] = own[n].astype(BF16)
        lower = lax.rem(lon, 4) < 2
        far_one[n] = jnp.where(lower, to_east[n], to_west[n]).astype(BF16)
        far_two[n] = jnp.where(lower, to_west[n], to_east[n]).astype(BF16)


def slot_base(owners, blocks, counts, k, block_count):
    lon = lax.axis_index("lon")
    size = lax.axis_size("lon")
    relative = lax.rem(owners[0, 0, k] - lon + 1 + size, size)
    base = (relative * block_count + blocks[0, 0, k]) * BLK
    return jnp.where(k < counts[0, 0], base, -(1 << 20))


def slot_targets(owners, blocks, counts, places, slot_count, block_count):
    slot = places // BLK
    target = places - slot * BLK
    for k in range(slot_count):
        base = slot_base(owners, blocks, counts, k, block_count)
        target = target + jnp.where(slot == k, base, 0)
    return target


def mask_row(mask):
    rows, cols = mask.shape
    cells = rows * cols
    spread = (iota((cols, cells), 1) % cols == iota((cols, cells), 0)).astype(BF16)
    wide = dot(mask.astype(F32).astype(BF16), spread)
    own = iota((rows, cells), 1) // cols == iota((rows, cells), 0)
    return jnp.sum(jnp.where(own, wide, 0.0), axis=0, keepdims=True)


def mask_column(mask):
    rows, cols = mask.shape
    cells = rows * cols
    spread = (iota((cells, rows), 0) // cols == iota((cells, rows), 1)).astype(BF16)
    wide = dot(spread, mask.astype(F32).astype(BF16))
    own = iota((cells, cols), 0) % cols == iota((cells, cols), 1)
    return jnp.sum(jnp.where(own, wide, 0.0), axis=1, keepdims=True)


def start_body(
    block_count,
    owners_in,
    blocks_in,
    counts,
    sea_in,
    tok_in,
    mask_in,
    projector_in,
    overlay_in,
    encoder_in,
    gain_in,
    lookup_in,
    lat_a,
    lat_b,
    to_core,
    to_chip,
    given,
    wanted,
    encoder,
    gain,
    tok,
    sea,
    lookup,
    mask,
    owners,
    blocks,
    projector,
    overlay,
    sems,
):
    lat_even = lax.rem(lax.axis_index("lat"), 2) == 0
    rows, cols, width = tok_in.shape
    sea_rows, _, channels = sea_in.shape
    tok_low = jnp.where(lat_even, rows - SHIFT, 0)
    tok_high = jnp.where(lat_even, 0, rows - SHIFT)
    sea_low = jnp.where(lat_even, sea_rows - HALF, 0)
    sea_high = jnp.where(lat_even, 0, sea_rows - HALF)
    moves = (
        (sea_in, sea),
        (projector_in, projector),
        (mask_in, mask),
        (overlay_in, overlay),
        (owners_in, owners),
        (blocks_in, blocks),
        (encoder_in, encoder),
        (gain_in, gain),
        (tok_in, tok),
        (lookup_in, lookup),
    )
    copies = [
        pltpu.make_async_copy(source, target, sems.at[n])
        for n, (source, target) in enumerate(moves)
    ]
    for copy in copies:
        copy.start()
    for copy in copies:
        copy.wait()
    count = SHIFT * cols
    lat_a[:count, :width] = tok[pl.ds(tok_low, SHIFT)].reshape(count, width)
    lat_b[:count, :width] = tok[pl.ds(tok_high, SHIFT)].reshape(count, width)
    lat_a[:count, width:] = sea[pl.ds(sea_low, HALF)].reshape(count, channels)
    lat_b[:count, width:] = sea[pl.ds(sea_high, HALF)].reshape(count, channels)
    put_columns(to_core, to_chip, 0, tok[...], SHIFT, slice(0, width))
    put_columns(to_core, to_chip, 0, sea[...], HALF, slice(width, width + channels))
    slot_count = overlay.shape[0] // BLK
    fields = projector.shape[0]
    patches = block_count * BLK
    cells = sea[...].reshape(-1, sea.shape[2])
    parts = jnp.concatenate(split3(projector[...]), axis=0).astype(BF16)
    spread = dot(parts, cells, ((1,), (1,)))
    values = spread[:fields] + spread[fields : 2 * fields] + spread[2 * fields :]
    values = (values * mask_row(mask[...])).astype(BF16)
    contrib = dot(values, overlay[...], ((1,), (1,)))
    stacked = jnp.concatenate(split3(contrib), axis=0).astype(BF16)
    shape = (slot_count * BLK, 3 * patches)
    places = iota((shape[0], 1), 0)
    target = slot_targets(owners, blocks, counts, places, slot_count, block_count)
    route = (iota(shape, 1) == target).astype(F32).astype(BF16)
    routed = dot(stacked, route)
    routed = routed[:fields] + routed[fields : 2 * fields] + routed[2 * fields :]
    parts = [routed[:, k * patches : (k + 1) * patches] for k in range(3)]
    low, high = [], []
    for n in range(2):
        for k in range(3):
            piece = split2(parts[k])[n]
            low.append(piece[:, patches - 128 :])
            high.append(piece[:, :128])
    given[...] = jnp.concatenate(parts, axis=0)
    wanted[...] = slot_targets(
        owners, blocks, counts, iota(wanted.shape, 1), slot_count, block_count
    )
    blank = jnp.zeros((8 - fields, 6 * 128), F32)
    low = jnp.concatenate([jnp.concatenate(low, axis=1), blank], axis=0)
    high = jnp.concatenate([jnp.concatenate(high, axis=1), blank], axis=0)
    lat_a[count:] = jnp.where(lat_even, low, high).astype(BF16)
    lat_b[count:] = jnp.where(lat_even, high, low).astype(BF16)


def attention_body(
    tok,
    from_a,
    from_b,
    side_core,
    side_chip,
    near_core,
    near_chip,
    far_one,
    far_two,
    sides,
    gain,
    weight,
    weight_bias,
    pos_bias,
    out_weight,
    projector,
    encoder,
    atm,
    flux,
    grid,
    fields_grid,
    key_mask,
    value_mask,
    mixed_rows,
    normed_rows,
    query_rows,
    value_rows,
    key_columns,
):
    rows, cols, width = tok.shape
    padded_rows, padded_cols = rows + 2 * SHIFT, cols + 2 * SHIFT
    band_count, per_band = padded_rows // WIN, padded_cols // WIN
    lat, lat_size = lax.axis_index("lat"), lax.axis_size("lat")
    lat_even = lax.rem(lat, 2) == 0
    lon_even = lax.rem(lax.axis_index("lon"), 2) == 0
    head = width // HEADS
    group = 128 // head
    places = WIN * WIN
    inner = slice(SHIFT, SHIFT + cols)

    def heads_match(shape, first, second):
        match = iota(shape, 0) // first == iota(shape, 1) // second
        return match.astype(F32).astype(BF16)

    key_mask[...] = heads_match(key_mask.shape, head, places)
    value_mask[...] = heads_match(value_mask.shape, places, head)

    fields = encoder.shape[0]
    lon = lax.axis_index("lon")
    span = sides.shape[1]

    def joined(ref, at, step):
        return ref[at, :, :span].astype(F32) + ref[at + step, :, :span].astype(F32)

    at = 2 * SHIFT
    west_side, east_side = pick(lon_even, joined(near_chip, at, 2), joined(near_core, at, 2))
    west_own, east_own = pick(lon_even, joined(near_chip, at + 1, 2), joined(near_core, at + 1, 2))
    lower = lax.rem(lon, 4) < 2
    far_west, far_east = pick(lower, joined(far_two, 0, 1), joined(far_one, 0, 1))
    to_west, own, to_east = [sides[k * fields : (k + 1) * fields] for k in range(3)]
    values = jnp.concatenate(
        [
            own + west_side + east_side,
            far_west + west_own + to_west,
            to_east + east_own + far_east,
            jnp.zeros_like(own),
        ],
        axis=0,
    )
    high, low = split2(values)
    turned = jnp.transpose(jnp.concatenate([high, low, high], axis=0))
    lanes = turned.shape[1]
    kind = (iota((1, 1, lanes), 2) % 16) // 4

    def put_fields(at, start, count):
        part = turned[start : start + count * cols].reshape(count, cols, lanes)
        fields_grid[at : at + count, inner, :lanes] = jnp.where(kind == 0, part, 0.0)
        fields_grid[at : at + count, :SHIFT, :lanes] = jnp.where(
            kind == 1, part[:, cols - SHIFT :], 0.0
        )
        fields_grid[at : at + count, SHIFT + cols :, :lanes] = jnp.where(
            kind == 2, part[:, :SHIFT], 0.0
        )

    put_fields(0, 128 - SHIFT * cols, SHIFT)
    put_fields(SHIFT, 128, rows)
    put_fields(SHIFT + rows, 128 + rows * cols, SHIFT)

    count = SHIFT * cols
    north, south = pick(lat_even, from_b[:count, :width], from_a[:count, :width])
    grid[SHIFT : SHIFT + rows, inner] = tok[...].astype(F32)
    grid[:SHIFT, inner] = north.astype(F32).reshape(SHIFT, cols, width)
    grid[SHIFT + rows :, inner] = south.astype(F32).reshape(SHIFT, cols, width)

    def lon_halos(west, east, far_west, far_east):
        for where, ref, corner in ((slice(0, SHIFT), west, far_west),
                                   (slice(SHIFT + cols, None), east, far_east)):
            grid[SHIFT : SHIFT + rows, where] = ref[:, :, :width].astype(F32)
            grid[:SHIFT, where] = corner[:SHIFT, :, :width].astype(F32)
            grid[SHIFT + rows :, where] = corner[SHIFT : 2 * SHIFT, :, :width].astype(F32)

    @pl.when(lon_even)
    def _():
        lon_halos(side_chip, side_core, near_chip, near_core)

    @pl.when(jnp.logical_not(lon_even))
    def _():
        lon_halos(side_core, side_chip, near_core, near_chip)

    enc = encoder[...]
    enc = jnp.concatenate([enc, enc, enc, jnp.zeros_like(enc)], axis=0)
    enc_high, enc_low = split2(enc)
    enc_stack = jnp.concatenate([enc_high, enc_high, enc_low], axis=0).astype(BF16)
    span = enc_stack.shape[0]
    lane = iota((places, HEADS * places), 1) % places
    crosses = (lane // (places // 2)) != (iota((places, HEADS * places), 0) // (places // 2))
    lane128 = iota((places, 2 * places), 1)
    band_rows = per_band * places

    def normalise(b, carry):
        at = pl.multiple_of(b * WIN, WIN)

        def windows(ref, lanes):
            return jnp.concatenate(
                [
                    ref[pl.ds(at, WIN), w * WIN : (w + 1) * WIN, :lanes].reshape(places, lanes)
                    for w in range(per_band)
                ],
                axis=0,
            )

        added = dot(windows(fields_grid, span).astype(BF16), enc_stack)
        mixed = (windows(grid, width) + added).astype(BF16)
        here = pl.ds(pl.multiple_of(b * band_rows, band_rows), band_rows)
        mixed_rows[here] = mixed
        mixed = mixed.astype(F32)
        average = jnp.mean(mixed, axis=-1, keepdims=True)
        centred = mixed - average
        spread = jnp.mean(centred * centred, axis=-1, keepdims=True)
        normed_rows[here] = (centred * lax.rsqrt(spread + 1e-05) * gain[...]).astype(BF16)
        return carry

    lax.fori_loop(0, band_count, normalise, 0)

    left = iota((256, 2 * places), 1) < places
    for at in range(0, 3 * width, 256):
        lanes = slice(at, at + 256)
        part = dot(normed_rows[...], weight[:, lanes]) + weight_bias[lanes].reshape(1, 256)
        if at < width:
            query_rows[:, lanes] = (part * head ** (-0.5)).astype(BF16)
        elif at >= 2 * width:
            value_rows[:, at - 2 * width : at - 2 * width + 256] = part.astype(BF16)
        else:
            turned = jnp.transpose(part)
            where = slice(at - width, at - width + 256)
            for n in range(0, band_count * per_band, 2):
                two = turned[:, n * places : (n + 2) * places]
                swapped = pltpu.roll(two, places, 1)
                at_n = 2 * n * places
                key_columns[where, at_n : at_n + 2 * places] = jnp.where(
                    left, two, swapped
                ).astype(BF16)
                at_n += 2 * places
                key_columns[where, at_n : at_n + 2 * places] = jnp.where(
                    left, swapped, two
                ).astype(BF16)

    groups = HEADS // group
    jobs = [(w, g) for w in range(per_band) for g in range(groups)]

    def attend(b, carry):
        start = b * band_rows
        first_band = jnp.logical_and(lat == 0, b == 0)
        last_band = jnp.logical_and(lat == lat_size - 1, b == band_count - 1)
        penalty = jnp.where(jnp.logical_or(first_band, last_band), -1000000000.0, 0.0)
        bias = pos_bias[...] + jnp.where(crosses, penalty, 0.0)
        keys_here, values_here = key_mask[...], value_mask[...]

        def place(job):
            w, g = job
            part = pl.ds(pl.multiple_of(start + w * places, places), places)
            return part, slice(g * group * head, (g + 1) * group * head)

        def scored(job):
            at = pl.multiple_of((b * per_band + job[0]) * 2 * places, 2 * places)
            part, lanes = place(job)
            k_wide = key_columns[lanes, pl.ds(at, 2 * places)]
            k_wide = jnp.concatenate([k_wide] * (group // 2), axis=1) * keys_here
            return dot(query_rows[part, lanes], k_wide)

        def weighted(job, scores):
            g = job[1]
            weights = []
            for pair in range(group // 2):
                at = pair * 2 * places
                s = scores[:, at : at + 2 * places]
                at += g * group * places
                s = s + bias[:, at : at + 2 * places]
                low = jnp.max(jnp.where(lane128 < places, s, -3e38), axis=1, keepdims=True)
                high = jnp.max(jnp.where(lane128 < places, -3e38, s), axis=1, keepdims=True)
                weights.append(jnp.exp(s - jnp.where(lane128 < places, low, high)))
            return jnp.concatenate(weights, axis=1).astype(BF16)

        def summed(job, expo):
            part, lanes = place(job)
            v_wide = jnp.concatenate([value_rows[part, lanes]] * group, axis=0) * values_here
            found = dot(expo, jnp.concatenate([v_wide, values_here], axis=1))
            size = group * head
            normed_rows[part, lanes] = (found[:, :size] / found[:, size:]).astype(BF16)

        scores, expos = {}, {}
        sets = [range(n, n + 4) for n in range(0, len(jobs), 4)]
        for t in range(len(sets) + 2):
            for n in sets[t] if t < len(sets) else ():
                scores[n] = scored(jobs[n])
            for n in sets[t - 2] if t >= 2 else ():
                summed(jobs[n], expos.pop(n))
            for n in sets[t - 1] if 0 <= t - 1 < len(sets) else ():
                expos[n] = weighted(jobs[n], scores.pop(n))
        return carry

    lax.fori_loop(0, band_count, attend, 0)

    for at in range(0, width, 256):
        lanes = slice(at, at + 256)
        projected = dot(normed_rows[...], out_weight[:, lanes]).astype(BF16).astype(F32)
        result = (mixed_rows[:, lanes].astype(F32) + projected).astype(BF16).astype(F32)
        for n in range(band_count * per_band):
            b, w = divmod(n, per_band)
            grid[b * WIN : (b + 1) * WIN, w * WIN : (w + 1) * WIN, lanes] = result[
                n * places : (n + 1) * places
            ].reshape(WIN, WIN, 256)
    own = grid[SHIFT : SHIFT + rows, inner]
    atm[...] = own.astype(BF16)
    flat = own.reshape(rows * cols, width).astype(BF16)
    flux[...] = dot(projector[...], flat, ((1,), (1,))).astype(BF16)


def conv_body(
    sea, from_a, from_b, side_core, side_chip, near_core, near_chip, kernel, bias, atm, conv, atm_out, grid, shifted, sem
):
    copy = pltpu.make_async_copy(atm, atm_out, sem)
    copy.start()
    lat_even = lax.rem(lax.axis_index("lat"), 2) == 0
    lon_even = lax.rem(lax.axis_index("lon"), 2) == 0
    rows, cols, channels = sea.shape
    width = from_a.shape[1] - channels
    inner = slice(HALF, HALF + cols)
    count = HALF * cols
    north, south = pick(lat_even, from_b[:count, width:], from_a[:count, width:])
    grid[HALF : HALF + rows, inner] = sea[...].astype(F32)
    grid[:HALF, inner] = north.astype(F32).reshape(HALF, cols, channels)
    grid[HALF + rows :, inner] = south.astype(F32).reshape(HALF, cols, channels)

    def lon_halos(west, east, far_west, far_east):
        for where, ref, corner in (
            (slice(0, HALF), west, far_west),
            (slice(HALF + cols, 2 * HALF + cols), east, far_east),
        ):
            grid[HALF : HALF + rows, where] = ref[:, :HALF, width:].astype(F32)
            grid[:HALF, where] = corner[:HALF, :HALF, width:].astype(F32)
            grid[HALF + rows :, where] = corner[SHIFT : SHIFT + HALF, :HALF, width:].astype(F32)

    @pl.when(lon_even)
    def _():
        lon_halos(side_chip, side_core, near_chip, near_core)

    @pl.when(jnp.logical_not(lon_even))
    def _():
        lon_halos(side_core, side_chip, near_core, near_chip)

    padded = grid.shape[1]
    for c in range(0, channels, 128):
        lanes = slice(c, c + 128)
        block = grid[:, :, lanes]
        for v in range(KER):
            turned = pltpu.roll(block, padded - v, 1) if v else block
            shifted[v] = turned[:, :cols]
        for s in range(0, cols, 8):
            total = jnp.broadcast_to(bias[:, lanes].reshape(1, 1, 128), (rows, 8, 128))
            for v in range(KER):
                column = shifted[v, :, s : s + 8]
                for u in range(KER):
                    tap = kernel[u, v : v + 1, lanes].reshape(1, 1, 128)
                    total = total + tap * column[u : u + rows]
            conv[:, s : s + 8, lanes] = total
    copy.wait()


def ocean_body(
    conv,
    flux,
    from_core,
    from_chip,
    route,
    overlay,
    encoder,
    gain,
    expand,
    contract,
    sea,
    wet,
    scale,
    out,
    done,
    sems,
):
    lon_even = lax.rem(lax.axis_index("lon"), 2) == 0
    west, east = pick(lon_even, from_chip[...], from_core[...])
    around = jnp.concatenate([west, flux[...], east], axis=1)
    picked = dot(around, route[...]).astype(BF16)
    forcing = dot(picked, overlay[...])
    high, low = split2(forcing)
    turned = jnp.transpose(jnp.concatenate([high, low, high], axis=0)).astype(BF16)
    enc_high, enc_low = split2(encoder[...])
    enc_stack = jnp.concatenate([enc_high, enc_high, enc_low], axis=0).astype(BF16)
    cells = out.shape[0]
    chunk = cells // 2
    copies = []
    for n, at in enumerate(range(0, cells, chunk)):
        part = slice(at, at + chunk)
        pre = conv[part] + dot(turned[part], enc_stack)
        average = jnp.mean(pre, axis=-1, keepdims=True)
        centred = pre - average
        spread = jnp.mean(centred * centred, axis=-1, keepdims=True)
        normed = (centred * lax.rsqrt(spread + 1e-06) * gain[...]).astype(BF16)
        hidden = dot(normed, expand[...])
        hidden = (0.5 * hidden * (1.0 + lax.erf(hidden * 0.5**0.5))).astype(BF16)
        update = dot(hidden, contract[...])
        kept = jnp.concatenate([wet[part]] * (update.shape[1] // 128), axis=1)
        done[part] = (sea[part].astype(F32) + kept * scale[...] * update).astype(BF16)
        copies.append(pltpu.make_async_copy(done.at[part], out.at[part], sems.at[n]))
        copies[-1].start()
    for copy in copies:
        copy.wait()


def tables_body(lookup, wanted, mask, out, route, wet):
    route[...] = (iota(route.shape, 0) == wanted[...]).astype(F32).astype(BF16)
    wet[...] = jnp.broadcast_to(mask_column(mask[...]), wet.shape)
    places = WIN * WIN
    span = 2 * WIN - 1
    width = 256
    entries = lookup.shape[1]
    flip = iota((entries, width), 0) + iota((entries, width), 1) == entries - 1
    parts = jnp.concatenate(split3(lookup[...]), axis=0).astype(BF16)
    parts = dot(parts, flip.astype(F32).astype(BF16))
    turned = parts[:HEADS] + parts[HEADS : 2 * HEADS] + parts[2 * HEADS :]
    middle = (WIN - 1) * (span + 1)
    row = iota((128, 2 * places), 0)
    lane = iota((128, 2 * places), 1) % places
    spread = (row == lane // WIN * span + lane % WIN).astype(F32).astype(BF16)
    spread = jnp.concatenate([spread] * 3, axis=0)
    half = iota((places, 2 * places), 1) < places
    for pair in range(HEADS // 2):
        found = []
        for h in (2 * pair, 2 * pair + 1):
            line = jnp.broadcast_to(turned[h : h + 1], (WIN, width))
            shifted = jnp.concatenate(
                [
                    pltpu.roll(
                        line, (width - middle + span * r) % width, 1, stride=1, stride_axis=0
                    )[:, :128]
                    for r in range(WIN)
                ],
                axis=0,
            )
            parts = jnp.concatenate(split3(shifted), axis=1).astype(BF16)
            found.append(dot(parts, spread))
        out[:, pair * 2 * places : (pair + 1) * 2 * places] = jnp.where(half, *found)


def local(
    atmos_patch_tokens,
    atmos_norm_gain,
    query_key_value_weight,
    query_key_value_bias,
    relative_bias_grid,
    attention_output_weight,
    flux_projector,
    surface_encoder,
    ocean_cell_state,
    land_sea_mask,
    depthwise_conv_kernel,
    depthwise_conv_bias,
    ocean_norm_gain,
    pointwise_expand,
    pointwise_contract,
    layer_update_scale,
    forcing_encoder,
    surface_projector,
    overlay_area_weight,
    owners,
    owner_tile_blocks,
    counts,
):
    lat_size, lon_size = lax.axis_size("lat"), lax.axis_size("lon")
    rows, cols, width = atmos_patch_tokens.shape
    sea_rows, sea_cols, channels = ocean_cell_state.shape
    cells = sea_rows * sea_cols
    patches = rows * cols
    block_count = patches // BLK
    slot_count = owners.shape[2]
    channel_count = flux_projector.shape[1]

    def swaps(pairs):
        return [(a, b) for a, b in pairs] + [(b, a) for a, b in pairs]

    lat_a = swaps([(k, k + 1) for k in range(0, lat_size - 1, 2)])
    lat_b = swaps([(k, k + 1) for k in range(1, lat_size - 1, 2)])
    core = swaps([(k, k + 1) for k in range(0, lon_size, 2)])
    chip = swaps([(k + 1, (k + 2) % lon_size) for k in range(0, lon_size, 2)])
    assert lon_size % 4 == 0
    lower = [k for k in range(lon_size) if k % 4 < 2]
    far_near = swaps([(k, k + 2) for k in lower])
    far_next = swaps([(k, (k - 2) % lon_size) for k in lower])

    tok, sea = atmos_patch_tokens, ocean_cell_state
    overlay = overlay_area_weight.reshape(slot_count * BLK, cells)
    fields = surface_projector.shape[1]
    lat_pack = struct((SHIFT * cols + 8, width + channels), BF16)
    side_pack = struct((rows, SHIFT, width + channels), BF16)
    firsts = (
        owners,
        owner_tile_blocks,
        counts,
        sea,
        tok,
        land_sea_mask,
        surface_projector.T,
        overlay,
        surface_encoder,
        atmos_norm_gain.reshape(1, width),
        relative_bias_grid,
    )

    def like(n):
        return struct(firsts[n].shape, firsts[n].dtype)

    firsts = tuple(
        x if n == 2 else pltpu.with_memory_space_constraint(x, pltpu.HBM)
        for n, x in enumerate(firsts)
    )
    to_a, to_b, to_core, to_chip, given, wanted, encoder, gain, tok, sea, lookup, mask = call(
        functools.partial(start_body, block_count),
        (lat_pack,) * 2
        + (side_pack,) * 2
        + (struct((3 * fields, patches), F32), struct((1, slot_count * BLK), jnp.int32))
        + (like(8), like(9), like(4), like(3), like(10), like(5)),
        firsts,
        specs=[smem() if n == 2 else anywhere() for n in range(len(firsts))],
        scratch=[pltpu.SMEM(x.shape, jnp.int32) for x in firsts[:2]]
        + [pltpu.VMEM(firsts[n].shape, firsts[n].dtype) for n in (6, 7)]
        + [pltpu.SemaphoreType.DMA((10,))],
        flops=3e8,
    )
    from_a = lax.ppermute(to_a, "lat", lat_a)
    from_b = lax.ppermute(to_b, "lat", lat_b)
    side_core = lax.ppermute(to_core, "lon", core)
    side_chip = lax.ppermute(to_chip, "lon", chip)

    near_pack = struct((2 * SHIFT + 4, SHIFT, width + channels), BF16)
    far_pack = struct((2, fields, patches + 256), BF16)
    to_core, to_chip, to_one, to_two, sides = call(
        functools.partial(pack_body, cols, width, sea_cols),
        (near_pack, near_pack, far_pack, far_pack, struct((3 * fields, patches + 256), F32)),
        (from_a, from_b, given),
    )
    near_core = lax.ppermute(to_core, "lon", core)
    near_chip = lax.ppermute(to_chip, "lon", chip)
    far_one = lax.ppermute(to_one, "lon", far_near)
    far_two = lax.ppermute(to_two, "lon", far_next)

    pos_bias, route, wet = call(
        tables_body,
        (
            struct((WIN * WIN, HEADS * WIN * WIN), F32),
            struct((3 * patches, slot_count * BLK), BF16),
            struct((cells, 128), F32),
        ),
        (lookup, wanted, mask),
        flops=5e8,
    )
    padded = (rows + 2 * SHIFT, cols + 2 * SHIFT)
    atm, flux = call(
        attention_body,
        (pltpu.VMEM((rows, cols, width), BF16), struct((channel_count, patches), BF16)),
        (
            tok,
            from_a,
            from_b,
            side_core,
            side_chip,
            near_core,
            near_chip,
            far_one,
            far_two,
            sides,
            gain,
            query_key_value_weight,
            query_key_value_bias,
            pos_bias,
            attention_output_weight,
            flux_projector.T,
            encoder,
        ),
        scratch=(
            pltpu.VMEM((*padded, width), F32),
            pltpu.VMEM((*padded, 128), F32),
            pltpu.VMEM((128, 128 * HEADS // width * WIN * WIN), BF16),
            pltpu.VMEM((128 * HEADS // width * WIN * WIN, 128), BF16),
            pltpu.VMEM((padded[0] * padded[1], width), BF16),
            pltpu.VMEM((padded[0] * padded[1], width), BF16),
            pltpu.VMEM((padded[0] * padded[1], width), BF16),
            pltpu.VMEM((padded[0] * padded[1], width), BF16),
            pltpu.VMEM((width, 2 * padded[0] * padded[1]), BF16),
        ),
        flops=3e9,
    )
    flux_core = lax.ppermute(flux, "lon", core)
    flux_chip = lax.ppermute(flux, "lon", chip)

    conv, atm = call(
        conv_body,
        (struct((sea_rows, sea_cols, channels), F32), struct((rows, cols, width), BF16)),
        (
            sea,
            from_a,
            from_b,
            side_core,
            side_chip,
            near_core,
            near_chip,
            depthwise_conv_kernel,
            depthwise_conv_bias.reshape(1, channels),
            atm,
        ),
        out_specs=[vmem(), anywhere()],
        scratch=(
            pltpu.VMEM((sea_rows + 2 * HALF, sea_cols + 8, channels), F32),
            pltpu.VMEM((KER, sea_rows + 2 * HALF, sea_cols, 128), F32),
            pltpu.SemaphoreType.DMA(()),
        ),
        flops=2e9,
    )
    (ocean,) = call(
        ocean_body,
        (struct((cells, channels), BF16),),
        (
            conv.reshape(cells, channels),
            flux,
            flux_core,
            flux_chip,
            route,
            overlay,
            forcing_encoder,
            ocean_norm_gain.reshape(1, channels),
            pointwise_expand,
            pointwise_contract,
            sea.reshape(cells, channels),
            wet,
            layer_update_scale.reshape(1, channels),
        ),
        out_specs=[anywhere()],
        scratch=[pltpu.VMEM((cells, channels), BF16), pltpu.SemaphoreType.DMA((2,))],
        flops=1e9,
    )
    return (atm, ocean.reshape(sea_rows, sea_cols, channels))


def solution(mesh):
    grid = P("lat", "lon", None)
    placed = (
        (grid,)
        + (P(),) * 7
        + (grid, P("lat", "lon"))
        + (P(),) * 8
        + (P("lat", "lon", None, None, None), grid, grid, P("lat", "lon"))
    )
    return jax.shard_map(
        local,
        mesh=mesh,
        in_specs=placed,
        out_specs=(grid, grid),
        check_vma=False,
    )
```

```python
import functools

import jax
import jax.numpy as jnp
from jax import lax
from jax.experimental import pallas as pl
from jax.experimental.pallas import tpu as pltpu
from jax.sharding import PartitionSpec as P


HEADS = 16
WIN = 8
SHIFT = 4
BLK = 64
KER = 7
HALF = KER // 2
F32 = jnp.float32
BF16 = jnp.bfloat16
VMEM_LIMIT = 48 * 1024 * 1024


def dot(a, b, dims=((1,), (0,))):
    return lax.dot_general(a, b, (dims, ((), ())), preferred_element_type=F32)


def iota(shape, dim):
    return lax.broadcasted_iota(jnp.int32, shape, dim)


def split2(x):
    high = x.astype(BF16)
    return high.astype(F32), (x - high.astype(F32)).astype(BF16).astype(F32)


def split3(x):
    high, rest = x.astype(BF16), x
    rest = rest - high.astype(F32)
    middle = rest.astype(BF16)
    return high.astype(F32), middle.astype(F32), rest - middle.astype(F32)


def pick(first_if, a, b):
    kind = a.dtype
    a, b = a.astype(F32), b.astype(F32)
    return (
        jnp.where(first_if, a, b).astype(kind),
        jnp.where(first_if, b, a).astype(kind),
    )


def vmem():
    return pl.BlockSpec(memory_space=pltpu.VMEM)


def smem():
    return pl.BlockSpec(memory_space=pltpu.SMEM)


def anywhere():
    return pl.BlockSpec(memory_space=pltpu.HBM)


def call(body, outs, args, specs=None, out_specs=None, scratch=(), flops=1e6):
    moved = sum(a.size * a.dtype.itemsize for a in args)
    return pl.pallas_call(
        body,
        out_shape=tuple(outs),
        in_specs=list(specs or [vmem()] * len(args)),
        out_specs=tuple(out_specs or [vmem()] * len(outs)),
        scratch_shapes=list(scratch),
        compiler_params=pltpu.CompilerParams(vmem_limit_bytes=VMEM_LIMIT),
        cost_estimate=pl.CostEstimate(
            flops=int(flops), bytes_accessed=int(moved), transcendentals=0
        ),
    )(*args)


def struct(shape, dtype):
    return jax.ShapeDtypeStruct(shape, dtype)


def lat_halos_of(lat_even, lat_a, lat_b, rows_cols, width, sea_cols):
    rows, cols = rows_cols
    count = rows * cols
    north, south = pick(lat_even, lat_b[:count], lat_a[:count])
    shape = (HALF, sea_cols, north.shape[1] - width)
    return (
        north[:, :width].reshape(rows, cols, width),
        south[:, :width].reshape(rows, cols, width),
        north[:, width:].reshape(shape),
        south[:, width:].reshape(shape),
    )


def put_columns(to_core, to_chip, at, values, count, lanes):
    lon_even = lax.rem(lax.axis_index("lon"), 2) == 0
    values = values.astype(F32)
    high, cols, _ = values.shape
    first, last = values[:, :count], values[:, cols - count :]
    to_core[at : at + high, :count, lanes] = jnp.where(lon_even, last, first).astype(BF16)
    to_chip[at : at + high, :count, lanes] = jnp.where(lon_even, first, last).astype(BF16)


def pack_body(
    cols, width, sea_cols, lat_a, lat_b, given, to_core, to_chip, far_one, far_two, sides
):
    fields = given.shape[0] // 3
    patches = given.shape[1]
    count = SHIFT * cols
    channels = lat_a.shape[1] - width
    lat_even = lax.rem(lax.axis_index("lat"), 2) == 0
    lon = lax.axis_index("lon")
    lon_even = lax.rem(lon, 2) == 0
    north, south, sea_north, sea_south = lat_halos_of(
        lat_even, lat_a, lat_b, (SHIFT, cols), width, sea_cols
    )
    lanes = slice(0, width)
    put_columns(to_core, to_chip, 0, north, SHIFT, lanes)
    put_columns(to_core, to_chip, SHIFT, south, SHIFT, lanes)
    lanes = slice(width, width + channels)
    put_columns(to_core, to_chip, 0, sea_north, HALF, lanes)
    put_columns(to_core, to_chip, SHIFT, sea_south, HALF, lanes)

    def pieces(ref):
        block = ref[count : count + 8].astype(F32)[:fields]
        return [
            block[:, 128 * k : 128 * k + 128] + block[:, 128 * (k + 3) : 128 * (k + 4)]
            for k in range(3)
        ]

    from_a, from_b = pieces(lat_a), pieces(lat_b)
    whole = []
    for k in range(3):
        whole.append(
            jnp.concatenate(
                [
                    jnp.where(lat_even, from_b[k], from_a[k]),
                    given[k * fields : (k + 1) * fields],
                    jnp.where(lat_even, from_a[k], from_b[k]),
                ],
                axis=1,
            )
        )
        sides[k * fields : (k + 1) * fields] = whole[k]
    to_west, own, to_east = [split2(w) for w in whole]
    span = patches + 256
    at = 2 * SHIFT
    for n in range(2):
        core_part = jnp.where(lon_even, to_east[n], to_west[n])
        chip_part = jnp.where(lon_even, to_west[n], to_east[n])
        to_core[at + 2 * n, :, :span] = core_part.astype(BF16)
        to_chip[at + 2 * n, :, :span] = chip_part.astype(BF16)
        to_core[at + 2 * n + 1, :, :span] = own[n].astype(BF16)
        to_chip[at + 2 * n + 1, :, :span] = own[n].astype(BF16)
        lower = lax.rem(lon, 4) < 2
        far_one[n] = jnp.where(lower, to_east[n], to_west[n]).astype(BF16)
        far_two[n] = jnp.where(lower, to_west[n], to_east[n]).astype(BF16)


def slot_base(owners, blocks, counts, k, block_count):
    lon = lax.axis_index("lon")
    size = lax.axis_size("lon")
    relative = lax.rem(owners[0, 0, k] - lon + 1 + size, size)
    base = (relative * block_count + blocks[0, 0, k]) * BLK
    return jnp.where(k < counts[0, 0], base, -(1 << 20))


def slot_targets(owners, blocks, counts, places, slot_count, block_count):
    slot = places // BLK
    target = places - slot * BLK
    for k in range(slot_count):
        base = slot_base(owners, blocks, counts, k, block_count)
        target = target + jnp.where(slot == k, base, 0)
    return target


def mask_row(mask):
    rows, cols = mask.shape
    cells = rows * cols
    spread = (iota((cols, cells), 1) % cols == iota((cols, cells), 0)).astype(BF16)
    wide = dot(mask.astype(F32).astype(BF16), spread)
    own = iota((rows, cells), 1) // cols == iota((rows, cells), 0)
    return jnp.sum(jnp.where(own, wide, 0.0), axis=0, keepdims=True)


def mask_column(mask):
    rows, cols = mask.shape
    cells = rows * cols
    spread = (iota((cells, rows), 0) // cols == iota((cells, rows), 1)).astype(BF16)
    wide = dot(spread, mask.astype(F32).astype(BF16))
    own = iota((cells, cols), 0) % cols == iota((cells, cols), 1)
    return jnp.sum(jnp.where(own, wide, 0.0), axis=1, keepdims=True)


def start_body(
    block_count,
    owners_in,
    blocks_in,
    counts,
    sea_in,
    tok_in,
    mask_in,
    projector_in,
    overlay_in,
    encoder_in,
    gain_in,
    lookup_in,
    lat_a,
    lat_b,
    to_core,
    to_chip,
    given,
    wanted,
    encoder,
    gain,
    tok,
    sea,
    lookup,
    mask,
    owners,
    blocks,
    projector,
    overlay,
    sems,
):
    lat_even = lax.rem(lax.axis_index("lat"), 2) == 0
    rows, cols, width = tok_in.shape
    sea_rows, _, channels = sea_in.shape
    tok_low = jnp.where(lat_even, rows - SHIFT, 0)
    tok_high = jnp.where(lat_even, 0, rows - SHIFT)
    sea_low = jnp.where(lat_even, sea_rows - HALF, 0)
    sea_high = jnp.where(lat_even, 0, sea_rows - HALF)
    moves = (
        (sea_in, sea),
        (projector_in, projector),
        (mask_in, mask),
        (overlay_in, overlay),
        (owners_in, owners),
        (blocks_in, blocks),
        (encoder_in, encoder),
        (gain_in, gain),
        (tok_in, tok),
        (lookup_in, lookup),
    )
    copies = {}
    for n, (source, target) in enumerate(moves):
        copy = pltpu.make_async_copy(source, target, sems.at[n])
        copy.start()
        copies[id(target)] = copy

    def ready(*targets):
        for target in targets:
            copies.pop(id(target)).wait()

    slot_count = overlay.shape[0] // BLK
    fields = projector.shape[0]
    patches = block_count * BLK
    shape = (slot_count * BLK, 3 * patches)
    ready(owners, blocks)
    places = iota((shape[0], 1), 0)
    target = slot_targets(owners, blocks, counts, places, slot_count, block_count)
    route = (iota(shape, 1) == target).astype(F32).astype(BF16)
    wanted[...] = slot_targets(
        owners, blocks, counts, iota(wanted.shape, 1), slot_count, block_count
    )
    ready(mask, projector, sea)
    parts = jnp.concatenate(split3(projector[...]), axis=0).astype(BF16)
    spread = dot(parts, sea[...].reshape(-1, channels), ((1,), (1,)))
    values = spread[:fields] + spread[fields : 2 * fields] + spread[2 * fields :]
    values = (values * mask_row(mask[...])).astype(BF16)
    put_columns(to_core, to_chip, 0, sea[...], HALF, slice(width, width + channels))
    ready(overlay, tok)
    contrib = dot(values, overlay[...], ((1,), (1,)))
    stacked = jnp.concatenate(split3(contrib), axis=0).astype(BF16)
    routed = dot(stacked, route)
    routed = routed[:fields] + routed[fields : 2 * fields] + routed[2 * fields :]
    count = SHIFT * cols
    lat_a[:count, :width] = tok[pl.ds(tok_low, SHIFT)].reshape(count, width)
    lat_b[:count, :width] = tok[pl.ds(tok_high, SHIFT)].reshape(count, width)
    lat_a[:count, width:] = sea[pl.ds(sea_low, HALF)].reshape(count, channels)
    lat_b[:count, width:] = sea[pl.ds(sea_high, HALF)].reshape(count, channels)
    put_columns(to_core, to_chip, 0, tok[...], SHIFT, slice(0, width))
    parts = [routed[:, k * patches : (k + 1) * patches] for k in range(3)]
    low, high = [], []
    for n in range(2):
        for k in range(3):
            piece = split2(parts[k])[n]
            low.append(piece[:, patches - 128 :])
            high.append(piece[:, :128])
    given[...] = jnp.concatenate(parts, axis=0)
    blank = jnp.zeros((8 - fields, 6 * 128), F32)
    low = jnp.concatenate([jnp.concatenate(low, axis=1), blank], axis=0)
    high = jnp.concatenate([jnp.concatenate(high, axis=1), blank], axis=0)
    lat_a[count:] = jnp.where(lat_even, low, high).astype(BF16)
    lat_b[count:] = jnp.where(lat_even, high, low).astype(BF16)
    ready(encoder, gain, lookup)


def prepare_body(tok, from_a, from_b, side_core, side_chip, grid):
    lat_even = lax.rem(lax.axis_index("lat"), 2) == 0
    lon_even = lax.rem(lax.axis_index("lon"), 2) == 0
    rows, cols, width = tok.shape
    count = SHIFT * cols
    inner = slice(SHIFT, SHIFT + cols)
    north, south = pick(lat_even, from_b[:count, :width], from_a[:count, :width])
    grid[SHIFT : SHIFT + rows, inner] = tok[...].astype(F32)
    grid[:SHIFT, inner] = north.astype(F32).reshape(SHIFT, cols, width)
    grid[SHIFT + rows :, inner] = south.astype(F32).reshape(SHIFT, cols, width)
    west, east = pick(lon_even, side_chip[:, :, :width], side_core[:, :, :width])
    blank = jnp.zeros((SHIFT, SHIFT, width), F32)
    for where, side in ((slice(0, SHIFT), west), (slice(SHIFT + cols, None), east)):
        grid[SHIFT : SHIFT + rows, where] = side.astype(F32)
        grid[:SHIFT, where] = blank
        grid[SHIFT + rows :, where] = blank


def attention_body(
    state,
    near_core,
    near_chip,
    far_one,
    far_two,
    sides,
    gain,
    weight,
    weight_bias,
    pos_bias,
    out_weight,
    projector,
    encoder,
    atm,
    flux,
    grid,
    fields_grid,
    corner,
    key_mask,
    value_mask,
    mixed_rows,
    normed_rows,
    query_rows,
    value_rows,
    key_columns,
):
    rows, cols, width = atm.shape
    padded_rows, padded_cols = rows + 2 * SHIFT, cols + 2 * SHIFT
    band_count, per_band = padded_rows // WIN, padded_cols // WIN
    lat, lat_size = lax.axis_index("lat"), lax.axis_size("lat")
    lat_even = lax.rem(lat, 2) == 0
    lon_even = lax.rem(lax.axis_index("lon"), 2) == 0
    head = width // HEADS
    group = 128 // head
    places = WIN * WIN
    inner = slice(SHIFT, SHIFT + cols)

    def heads_match(shape, first, second):
        match = iota(shape, 0) // first == iota(shape, 1) // second
        return match.astype(F32).astype(BF16)

    key_mask[...] = heads_match(key_mask.shape, head, places)
    value_mask[...] = heads_match(value_mask.shape, places, head)

    fields = encoder.shape[0]
    lon = lax.axis_index("lon")
    span = sides.shape[1]

    def joined(ref, at, step):
        return ref[at, :, :span].astype(F32) + ref[at + step, :, :span].astype(F32)

    at = 2 * SHIFT
    west_side, east_side = pick(lon_even, joined(near_chip, at, 2), joined(near_core, at, 2))
    west_own, east_own = pick(lon_even, joined(near_chip, at + 1, 2), joined(near_core, at + 1, 2))
    lower = lax.rem(lon, 4) < 2
    far_west, far_east = pick(lower, joined(far_two, 0, 1), joined(far_one, 0, 1))
    to_west, own, to_east = [sides[k * fields : (k + 1) * fields] for k in range(3)]
    values = jnp.concatenate(
        [
            own + west_side + east_side,
            far_west + west_own + to_west,
            to_east + east_own + far_east,
            jnp.zeros_like(own),
        ],
        axis=0,
    )
    high, low = split2(values)
    turned = jnp.transpose(jnp.concatenate([high, low, high], axis=0))
    lanes = turned.shape[1]
    kind = (iota((1, 1, lanes), 2) % 16) // 4

    def put_fields(at, start, count):
        part = turned[start : start + count * cols].reshape(count, cols, lanes)
        fields_grid[at : at + count, inner, :lanes] = jnp.where(kind == 0, part, 0.0)
        fields_grid[at : at + count, :SHIFT, :lanes] = jnp.where(
            kind == 1, part[:, cols - SHIFT :], 0.0
        )
        fields_grid[at : at + count, SHIFT + cols :, :lanes] = jnp.where(
            kind == 2, part[:, :SHIFT], 0.0
        )

    put_fields(0, 128 - SHIFT * cols, SHIFT)
    put_fields(SHIFT, 128, rows)
    put_fields(SHIFT + rows, 128 + rows * cols, SHIFT)

    def corners(west, east):
        corner[...] = jnp.zeros(corner.shape, F32)
        last = band_count - 1
        corner[0, 0, :SHIFT, :SHIFT] = west[:SHIFT, :, :width].astype(F32)
        corner[0, 1, :SHIFT, WIN - SHIFT :] = east[:SHIFT, :, :width].astype(F32)
        corner[last, 0, WIN - SHIFT :, :SHIFT] = west[SHIFT : 2 * SHIFT, :, :width].astype(F32)
        corner[last, 1, WIN - SHIFT :, WIN - SHIFT :] = east[
            SHIFT : 2 * SHIFT, :, :width
        ].astype(F32)

    @pl.when(lon_even)
    def _():
        corners(near_chip, near_core)

    @pl.when(jnp.logical_not(lon_even))
    def _():
        corners(near_core, near_chip)

    enc = encoder[...]
    enc = jnp.concatenate([enc, enc, enc, jnp.zeros_like(enc)], axis=0)
    enc_high, enc_low = split2(enc)
    enc_stack = jnp.concatenate([enc_high, enc_high, enc_low], axis=0).astype(BF16)
    span = enc_stack.shape[0]
    lane = iota((places, HEADS * places), 1) % places
    crosses = (lane // (places // 2)) != (iota((places, HEADS * places), 0) // (places // 2))
    lane128 = iota((places, 2 * places), 1)
    band_rows = per_band * places

    def normalise(b, carry):
        at = pl.multiple_of(b * WIN, WIN)

        fields_here = [
            fields_grid[pl.ds(at, WIN), w * WIN : (w + 1) * WIN, :span].reshape(places, span)
            for w in range(per_band)
        ]
        added = dot(jnp.concatenate(fields_here, axis=0).astype(BF16), enc_stack)
        held = [
            state[pl.ds(at, WIN), w * WIN : (w + 1) * WIN].reshape(places, width)
            for w in range(per_band)
        ]
        held[0] = held[0] + corner[b, 0].reshape(places, width)
        held[-1] = held[-1] + corner[b, 1].reshape(places, width)
        mixed = (jnp.concatenate(held, axis=0) + added).astype(BF16)
        here = pl.ds(pl.multiple_of(b * band_rows, band_rows), band_rows)
        mixed_rows[here] = mixed
        mixed = mixed.astype(F32)
        average = jnp.mean(mixed, axis=-1, keepdims=True)
        centred = mixed - average
        spread = jnp.mean(centred * centred, axis=-1, keepdims=True)
        normed_rows[here] = (centred * lax.rsqrt(spread + 1e-05) * gain[...]).astype(BF16)
        return carry

    lax.fori_loop(0, band_count, normalise, 0, unroll=True)

    left = iota((256, 2 * places), 1) < places
    keys_first = [(at + width) % (3 * width) for at in range(0, 3 * width, 256)]
    for at in keys_first:
        lanes = slice(at, at + 256)
        part = dot(normed_rows[...], weight[:, lanes]) + weight_bias[lanes].reshape(1, 256)
        if at < width:
            query_rows[:, lanes] = (part * head ** (-0.5)).astype(BF16)
        elif at >= 2 * width:
            value_rows[:, at - 2 * width : at - 2 * width + 256] = part.astype(BF16)
        else:
            turned = jnp.transpose(part)
            where = slice(at - width, at - width + 256)
            for n in range(0, band_count * per_band, 2):
                two = turned[:, n * places : (n + 2) * places]
                swapped = pltpu.roll(two, places, 1)
                at_n = 2 * n * places
                key_columns[where, at_n : at_n + 2 * places] = jnp.where(
                    left, two, swapped
                ).astype(BF16)
                at_n += 2 * places
                key_columns[where, at_n : at_n + 2 * places] = jnp.where(
                    left, swapped, two
                ).astype(BF16)

    groups = HEADS // group
    jobs = [(w, g) for w in range(per_band) for g in range(groups)]

    def attend(b, carry):
        start = b * band_rows
        first_band = jnp.logical_and(lat == 0, b == 0)
        last_band = jnp.logical_and(lat == lat_size - 1, b == band_count - 1)
        penalty = jnp.where(jnp.logical_or(first_band, last_band), -1000000000.0, 0.0)
        bias = pos_bias[...] + jnp.where(crosses, penalty, 0.0)
        keys_here, values_here = key_mask[...], value_mask[...]

        def place(job):
            w, g = job
            part = pl.ds(pl.multiple_of(start + w * places, places), places)
            return part, slice(g * group * head, (g + 1) * group * head)

        def scored(job):
            at = pl.multiple_of((b * per_band + job[0]) * 2 * places, 2 * places)
            part, lanes = place(job)
            k_wide = key_columns[lanes, pl.ds(at, 2 * places)]
            k_wide = jnp.concatenate([k_wide] * (group // 2), axis=1) * keys_here
            return dot(query_rows[part, lanes], k_wide)

        def weighted(job, scores):
            g = job[1]
            weights = []
            for pair in range(group // 2):
                at = pair * 2 * places
                s = scores[:, at : at + 2 * places]
                at += g * group * places
                s = s + bias[:, at : at + 2 * places]
                low = jnp.max(jnp.where(lane128 < places, s, -3e38), axis=1, keepdims=True)
                high = jnp.max(jnp.where(lane128 < places, -3e38, s), axis=1, keepdims=True)
                weights.append(jnp.exp(s - jnp.where(lane128 < places, low, high)))
            return jnp.concatenate(weights, axis=1).astype(BF16)

        def summed(job, expo):
            part, lanes = place(job)
            v_wide = jnp.concatenate([value_rows[part, lanes]] * group, axis=0) * values_here
            found = dot(expo, jnp.concatenate([v_wide, values_here], axis=1))
            size = group * head
            normed_rows[part, lanes] = (found[:, :size] / found[:, size:]).astype(BF16)

        scores, expos = {}, {}
        sets = [range(n, n + 4) for n in range(0, len(jobs), 4)]
        for t in range(len(sets) + 2):
            for n in sets[t] if t < len(sets) else ():
                scores[n] = scored(jobs[n])
            for n in sets[t - 2] if t >= 2 else ():
                summed(jobs[n], expos.pop(n))
            for n in sets[t - 1] if 0 <= t - 1 < len(sets) else ():
                expos[n] = weighted(jobs[n], scores.pop(n))
        return carry

    lax.fori_loop(0, band_count, attend, 0, unroll=True)

    for at in range(0, width, 256):
        lanes = slice(at, at + 256)
        projected = dot(normed_rows[...], out_weight[:, lanes]).astype(BF16).astype(F32)
        result = (mixed_rows[:, lanes].astype(F32) + projected).astype(BF16).astype(F32)
        for n in range(band_count * per_band):
            b, w = divmod(n, per_band)
            grid[b * WIN : (b + 1) * WIN, w * WIN : (w + 1) * WIN, lanes] = result[
                n * places : (n + 1) * places
            ].reshape(WIN, WIN, 256)
    own = grid[SHIFT : SHIFT + rows, inner]
    atm[...] = own.astype(BF16)
    flat = own.reshape(rows * cols, width).astype(BF16)
    flux[...] = dot(projector[...], flat, ((1,), (1,))).astype(BF16)


def conv_body(
    sea, from_a, from_b, side_core, side_chip, near_core, near_chip, kernel, bias, atm, conv, atm_out, grid, shifted, sem
):
    copy = pltpu.make_async_copy(atm, atm_out, sem)
    copy.start()
    lat_even = lax.rem(lax.axis_index("lat"), 2) == 0
    lon_even = lax.rem(lax.axis_index("lon"), 2) == 0
    rows, cols, channels = sea.shape
    width = from_a.shape[1] - channels
    inner = slice(HALF, HALF + cols)
    count = HALF * cols
    north, south = pick(lat_even, from_b[:count, width:], from_a[:count, width:])
    grid[HALF : HALF + rows, inner] = sea[...].astype(F32)
    grid[:HALF, inner] = north.astype(F32).reshape(HALF, cols, channels)
    grid[HALF + rows :, inner] = south.astype(F32).reshape(HALF, cols, channels)

    def lon_halos(west, east, far_west, far_east):
        for where, ref, corner in (
            (slice(0, HALF), west, far_west),
            (slice(HALF + cols, 2 * HALF + cols), east, far_east),
        ):
            grid[HALF : HALF + rows, where] = ref[:, :HALF, width:].astype(F32)
            grid[:HALF, where] = corner[:HALF, :HALF, width:].astype(F32)
            grid[HALF + rows :, where] = corner[SHIFT : SHIFT + HALF, :HALF, width:].astype(F32)

    @pl.when(lon_even)
    def _():
        lon_halos(side_chip, side_core, near_chip, near_core)

    @pl.when(jnp.logical_not(lon_even))
    def _():
        lon_halos(side_core, side_chip, near_core, near_chip)

    padded = grid.shape[1]
    for c in range(0, channels, 128):
        lanes = slice(c, c + 128)
        block = grid[:, :, lanes]
        for v in range(KER):
            turned = pltpu.roll(block, padded - v, 1) if v else block
            shifted[v] = turned[:, :cols]
        for s in range(0, cols, 8):
            total = jnp.broadcast_to(bias[:, lanes].reshape(1, 1, 128), (rows, 8, 128))
            for v in range(KER):
                column = shifted[v, :, s : s + 8]
                for u in range(KER):
                    tap = kernel[u, v : v + 1, lanes].reshape(1, 1, 128)
                    total = total + tap * column[u : u + rows]
            conv[:, s : s + 8, lanes] = total
    copy.wait()


def ocean_body(
    conv,
    flux,
    from_core,
    from_chip,
    route,
    overlay,
    encoder,
    gain,
    expand,
    contract,
    sea,
    wet,
    scale,
    out,
):
    lon_even = lax.rem(lax.axis_index("lon"), 2) == 0
    west, east = pick(lon_even, from_chip[...], from_core[...])
    around = jnp.concatenate([west, flux[...], east], axis=1)
    picked = dot(around, route[...]).astype(BF16)
    forcing = dot(picked, overlay[...])
    high, low = split2(forcing)
    turned = jnp.transpose(jnp.concatenate([high, low, high], axis=0)).astype(BF16)
    enc_high, enc_low = split2(encoder[...])
    enc_stack = jnp.concatenate([enc_high, enc_high, enc_low], axis=0).astype(BF16)
    pre = conv[...] + dot(turned, enc_stack)
    average = jnp.mean(pre, axis=-1, keepdims=True)
    centred = pre - average
    spread = jnp.mean(centred * centred, axis=-1, keepdims=True)
    normed = (centred * lax.rsqrt(spread + 1e-06) * gain[...]).astype(BF16)
    hidden = dot(normed, expand[...])
    hidden = (0.5 * hidden * (1.0 + lax.erf(hidden * 0.5**0.5))).astype(BF16)
    update = dot(hidden, contract[...])
    kept = jnp.concatenate([wet[...]] * (update.shape[1] // 128), axis=1)
    out[...] = (sea[...].astype(F32) + kept * scale[...] * update).astype(BF16)


def tables_body(lookup, wanted, mask, out, route, wet):
    route[...] = (iota(route.shape, 0) == wanted[...]).astype(F32).astype(BF16)
    wet[...] = jnp.broadcast_to(mask_column(mask[...]), wet.shape)
    places = WIN * WIN
    span = 2 * WIN - 1
    width = 256
    entries = lookup.shape[1]
    flip = iota((entries, width), 0) + iota((entries, width), 1) == entries - 1
    parts = jnp.concatenate(split3(lookup[...]), axis=0).astype(BF16)
    parts = dot(parts, flip.astype(F32).astype(BF16))
    turned = parts[:HEADS] + parts[HEADS : 2 * HEADS] + parts[2 * HEADS :]
    middle = (WIN - 1) * (span + 1)
    row = iota((128, 2 * places), 0)
    lane = iota((128, 2 * places), 1) % places
    spread = (row == lane // WIN * span + lane % WIN).astype(F32).astype(BF16)
    spread = jnp.concatenate([spread] * 3, axis=0)
    half = iota((places, 2 * places), 1) < places
    for pair in range(HEADS // 2):
        found = []
        for h in (2 * pair, 2 * pair + 1):
            line = jnp.broadcast_to(turned[h : h + 1], (WIN, width))
            shifted = jnp.concatenate(
                [
                    pltpu.roll(
                        line, (width - middle + span * r) % width, 1, stride=1, stride_axis=0
                    )[:, :128]
                    for r in range(WIN)
                ],
                axis=0,
            )
            parts = jnp.concatenate(split3(shifted), axis=1).astype(BF16)
            found.append(dot(parts, spread))
        out[:, pair * 2 * places : (pair + 1) * 2 * places] = jnp.where(half, *found)


def local(
    atmos_patch_tokens,
    atmos_norm_gain,
    query_key_value_weight,
    query_key_value_bias,
    relative_bias_grid,
    attention_output_weight,
    flux_projector,
    surface_encoder,
    ocean_cell_state,
    land_sea_mask,
    depthwise_conv_kernel,
    depthwise_conv_bias,
    ocean_norm_gain,
    pointwise_expand,
    pointwise_contract,
    layer_update_scale,
    forcing_encoder,
    surface_projector,
    overlay_area_weight,
    owners,
    owner_tile_blocks,
    counts,
):
    lat_size, lon_size = lax.axis_size("lat"), lax.axis_size("lon")
    rows, cols, width = atmos_patch_tokens.shape
    sea_rows, sea_cols, channels = ocean_cell_state.shape
    cells = sea_rows * sea_cols
    patches = rows * cols
    block_count = patches // BLK
    slot_count = owners.shape[2]
    channel_count = flux_projector.shape[1]

    def swaps(pairs):
        return [(a, b) for a, b in pairs] + [(b, a) for a, b in pairs]

    lat_a = swaps([(k, k + 1) for k in range(0, lat_size - 1, 2)])
    lat_b = swaps([(k, k + 1) for k in range(1, lat_size - 1, 2)])
    core = swaps([(k, k + 1) for k in range(0, lon_size, 2)])
    chip = swaps([(k + 1, (k + 2) % lon_size) for k in range(0, lon_size, 2)])
    assert lon_size % 4 == 0
    lower = [k for k in range(lon_size) if k % 4 < 2]
    far_near = swaps([(k, k + 2) for k in lower])
    far_next = swaps([(k, (k - 2) % lon_size) for k in lower])

    tok, sea = atmos_patch_tokens, ocean_cell_state
    overlay = overlay_area_weight.reshape(slot_count * BLK, cells)
    fields = surface_projector.shape[1]
    lat_pack = struct((SHIFT * cols + 8, width + channels), BF16)
    side_pack = struct((rows, SHIFT, width + channels), BF16)
    firsts = (
        owners,
        owner_tile_blocks,
        counts,
        sea,
        tok,
        land_sea_mask,
        surface_projector.T,
        overlay,
        surface_encoder,
        atmos_norm_gain.reshape(1, width),
        relative_bias_grid,
    )

    def like(n):
        return struct(firsts[n].shape, firsts[n].dtype)

    firsts = tuple(
        x if n == 2 else pltpu.with_memory_space_constraint(x, pltpu.HBM)
        for n, x in enumerate(firsts)
    )
    to_a, to_b, to_core, to_chip, given, wanted, encoder, gain, tok, sea, lookup, mask = call(
        functools.partial(start_body, block_count),
        (lat_pack,) * 2
        + (side_pack,) * 2
        + (struct((3 * fields, patches), F32), struct((1, slot_count * BLK), jnp.int32))
        + (like(8), like(9), like(4), like(3), like(10), like(5)),
        firsts,
        specs=[smem() if n == 2 else anywhere() for n in range(len(firsts))],
        scratch=[pltpu.SMEM(x.shape, jnp.int32) for x in firsts[:2]]
        + [pltpu.VMEM(firsts[n].shape, firsts[n].dtype) for n in (6, 7)]
        + [pltpu.SemaphoreType.DMA((10,))],
        flops=3e8,
    )
    from_a = lax.ppermute(to_a, "lat", lat_a)
    from_b = lax.ppermute(to_b, "lat", lat_b)
    side_core = lax.ppermute(to_core, "lon", core)
    side_chip = lax.ppermute(to_chip, "lon", chip)

    near_pack = struct((2 * SHIFT + 4, SHIFT, width + channels), BF16)
    far_pack = struct((2, fields, patches + 256), BF16)
    to_core, to_chip, to_one, to_two, sides = call(
        functools.partial(pack_body, cols, width, sea_cols),
        (near_pack, near_pack, far_pack, far_pack, struct((3 * fields, patches + 256), F32)),
        (from_a, from_b, given),
    )
    near_core = lax.ppermute(to_core, "lon", core)
    near_chip = lax.ppermute(to_chip, "lon", chip)
    far_one = lax.ppermute(to_one, "lon", far_near)
    far_two = lax.ppermute(to_two, "lon", far_next)

    pos_bias, route, wet = call(
        tables_body,
        (
            struct((WIN * WIN, HEADS * WIN * WIN), F32),
            struct((3 * patches, slot_count * BLK), BF16),
            struct((cells, 128), F32),
        ),
        (lookup, wanted, mask),
        flops=5e8,
    )
    padded = (rows + 2 * SHIFT, cols + 2 * SHIFT)
    (state,) = call(
        prepare_body,
        (pltpu.VMEM((*padded, width), F32),),
        (tok, from_a, from_b, side_core, side_chip),
    )
    atm, flux = call(
        attention_body,
        (pltpu.VMEM((rows, cols, width), BF16), struct((channel_count, patches), BF16)),
        (
            state,
            near_core,
            near_chip,
            far_one,
            far_two,
            sides,
            gain,
            query_key_value_weight,
            query_key_value_bias,
            pos_bias,
            attention_output_weight,
            flux_projector.T,
            encoder,
        ),
        scratch=(
            pltpu.VMEM((*padded, width), F32),
            pltpu.VMEM((*padded, 128), F32),
            pltpu.VMEM((padded[0] // WIN, 2, WIN, WIN, width), F32),
            pltpu.VMEM((128, 128 * HEADS // width * WIN * WIN), BF16),
            pltpu.VMEM((128 * HEADS // width * WIN * WIN, 128), BF16),
            pltpu.VMEM((padded[0] * padded[1], width), BF16),
            pltpu.VMEM((padded[0] * padded[1], width), BF16),
            pltpu.VMEM((padded[0] * padded[1], width), BF16),
            pltpu.VMEM((padded[0] * padded[1], width), BF16),
            pltpu.VMEM((width, 2 * padded[0] * padded[1]), BF16),
        ),
        flops=3e9,
    )
    flux_core = lax.ppermute(flux, "lon", core)
    flux_chip = lax.ppermute(flux, "lon", chip)

    conv, atm = call(
        conv_body,
        (struct((sea_rows, sea_cols, channels), F32), struct((rows, cols, width), BF16)),
        (
            sea,
            from_a,
            from_b,
            side_core,
            side_chip,
            near_core,
            near_chip,
            depthwise_conv_kernel,
            depthwise_conv_bias.reshape(1, channels),
            atm,
        ),
        out_specs=[vmem(), anywhere()],
        scratch=(
            pltpu.VMEM((sea_rows + 2 * HALF, sea_cols + 8, channels), F32),
            pltpu.VMEM((KER, sea_rows + 2 * HALF, sea_cols, 128), F32),
            pltpu.SemaphoreType.DMA(()),
        ),
        flops=2e9,
    )
    (ocean,) = call(
        ocean_body,
        (struct((cells, channels), BF16),),
        (
            conv.reshape(cells, channels),
            flux,
            flux_core,
            flux_chip,
            route,
            overlay,
            forcing_encoder,
            ocean_norm_gain.reshape(1, channels),
            pointwise_expand,
            pointwise_contract,
            sea.reshape(cells, channels),
            wet,
            layer_update_scale.reshape(1, channels),
        ),
        flops=1e9,
    )
    return (atm, ocean.reshape(sea_rows, sea_cols, channels))


def solution(mesh):
    grid = P("lat", "lon", None)
    placed = (
        (grid,)
        + (P(),) * 7
        + (grid, P("lat", "lon"))
        + (P(),) * 8
        + (P("lat", "lon", None, None, None), grid, grid, P("lat", "lon"))
    )
    return jax.shard_map(
        local,
        mesh=mesh,
        in_specs=placed,
        out_specs=(grid, grid),
        check_vma=False,
    )
```

```python
import functools

import jax
import jax.numpy as jnp
from jax import lax
from jax.experimental import pallas as pl
from jax.experimental.pallas import tpu as pltpu
from jax.sharding import PartitionSpec as P


HEADS = 16
WIN = 8
SHIFT = 4
BLK = 64
KER = 7
HALF = KER // 2
F32 = jnp.float32
BF16 = jnp.bfloat16
VMEM_LIMIT = 48 * 1024 * 1024


def dot(a, b, dims=((1,), (0,))):
    return lax.dot_general(a, b, (dims, ((), ())), preferred_element_type=F32)


def iota(shape, dim):
    return lax.broadcasted_iota(jnp.int32, shape, dim)


def split2(x):
    high = x.astype(BF16)
    return high.astype(F32), (x - high.astype(F32)).astype(BF16).astype(F32)


def split3(x):
    high, rest = x.astype(BF16), x
    rest = rest - high.astype(F32)
    middle = rest.astype(BF16)
    return high.astype(F32), middle.astype(F32), rest - middle.astype(F32)


def pick(first_if, a, b):
    kind = a.dtype
    a, b = a.astype(F32), b.astype(F32)
    return (
        jnp.where(first_if, a, b).astype(kind),
        jnp.where(first_if, b, a).astype(kind),
    )


def vmem():
    return pl.BlockSpec(memory_space=pltpu.VMEM)


def smem():
    return pl.BlockSpec(memory_space=pltpu.SMEM)


def anywhere():
    return pl.BlockSpec(memory_space=pltpu.HBM)


def call(body, outs, args, specs=None, out_specs=None, scratch=(), flops=1e6):
    moved = sum(a.size * a.dtype.itemsize for a in args)
    return pl.pallas_call(
        body,
        out_shape=tuple(outs),
        in_specs=list(specs or [vmem()] * len(args)),
        out_specs=tuple(out_specs or [vmem()] * len(outs)),
        scratch_shapes=list(scratch),
        compiler_params=pltpu.CompilerParams(vmem_limit_bytes=VMEM_LIMIT),
        cost_estimate=pl.CostEstimate(
            flops=int(flops), bytes_accessed=int(moved), transcendentals=0
        ),
    )(*args)


def struct(shape, dtype):
    return jax.ShapeDtypeStruct(shape, dtype)


def lat_halos_of(lat_even, lat_a, lat_b, rows_cols, width, sea_cols):
    rows, cols = rows_cols
    count = rows * cols
    north, south = pick(lat_even, lat_b[:count], lat_a[:count])
    shape = (HALF, sea_cols, north.shape[1] - width)
    return (
        north[:, :width].reshape(rows, cols, width),
        south[:, :width].reshape(rows, cols, width),
        north[:, width:].reshape(shape),
        south[:, width:].reshape(shape),
    )


def put_columns(to_core, to_chip, at, values, count, lanes):
    lon_even = lax.rem(lax.axis_index("lon"), 2) == 0
    values = values.astype(F32)
    high, cols, _ = values.shape
    first, last = values[:, :count], values[:, cols - count :]
    to_core[at : at + high, :count, lanes] = jnp.where(lon_even, last, first).astype(BF16)
    to_chip[at : at + high, :count, lanes] = jnp.where(lon_even, first, last).astype(BF16)


def pack_body(
    cols, width, sea_cols, lat_a, lat_b, given, to_core, to_chip, far_one, far_two, sides
):
    fields = given.shape[0] // 3
    patches = given.shape[1]
    count = SHIFT * cols
    channels = lat_a.shape[1] - width
    lat_even = lax.rem(lax.axis_index("lat"), 2) == 0
    lon = lax.axis_index("lon")
    lon_even = lax.rem(lon, 2) == 0
    north, south, sea_north, sea_south = lat_halos_of(
        lat_even, lat_a, lat_b, (SHIFT, cols), width, sea_cols
    )
    lanes = slice(0, width)
    put_columns(to_core, to_chip, 0, north, SHIFT, lanes)
    put_columns(to_core, to_chip, SHIFT, south, SHIFT, lanes)
    lanes = slice(width, width + channels)
    put_columns(to_core, to_chip, 0, sea_north, HALF, lanes)
    put_columns(to_core, to_chip, SHIFT, sea_south, HALF, lanes)

    def pieces(ref):
        block = ref[count : count + 8].astype(F32)[:fields]
        return [
            block[:, 128 * k : 128 * k + 128] + block[:, 128 * (k + 3) : 128 * (k + 4)]
            for k in range(3)
        ]

    from_a, from_b = pieces(lat_a), pieces(lat_b)
    whole = []
    for k in range(3):
        whole.append(
            jnp.concatenate(
                [
                    jnp.where(lat_even, from_b[k], from_a[k]),
                    given[k * fields : (k + 1) * fields],
                    jnp.where(lat_even, from_a[k], from_b[k]),
                ],
                axis=1,
            )
        )
        sides[k * fields : (k + 1) * fields] = whole[k]
    to_west, own, to_east = [split2(w) for w in whole]
    span = patches + 256
    at = 2 * SHIFT
    for n in range(2):
        core_part = jnp.where(lon_even, to_east[n], to_west[n])
        chip_part = jnp.where(lon_even, to_west[n], to_east[n])
        to_core[at + 2 * n, :, :span] = core_part.astype(BF16)
        to_chip[at + 2 * n, :, :span] = chip_part.astype(BF16)
        to_core[at + 2 * n + 1, :, :span] = own[n].astype(BF16)
        to_chip[at + 2 * n + 1, :, :span] = own[n].astype(BF16)
        lower = lax.rem(lon, 4) < 2
        far_one[n] = jnp.where(lower, to_east[n], to_west[n]).astype(BF16)
        far_two[n] = jnp.where(lower, to_west[n], to_east[n]).astype(BF16)


def slot_base(owners, blocks, counts, k, block_count):
    lon = lax.axis_index("lon")
    size = lax.axis_size("lon")
    relative = lax.rem(owners[0, 0, k] - lon + 1 + size, size)
    base = (relative * block_count + blocks[0, 0, k]) * BLK
    return jnp.where(k < counts[0, 0], base, -(1 << 20))


def slot_targets(owners, blocks, counts, places, slot_count, block_count):
    slot = places // BLK
    target = places - slot * BLK
    for k in range(slot_count):
        base = slot_base(owners, blocks, counts, k, block_count)
        target = target + jnp.where(slot == k, base, 0)
    return target


def mask_row(mask):
    rows, cols = mask.shape
    cells = rows * cols
    spread = (iota((cols, cells), 1) % cols == iota((cols, cells), 0)).astype(BF16)
    wide = dot(mask.astype(F32).astype(BF16), spread)
    own = iota((rows, cells), 1) // cols == iota((rows, cells), 0)
    return jnp.sum(jnp.where(own, wide, 0.0), axis=0, keepdims=True)


def mask_column(mask):
    rows, cols = mask.shape
    cells = rows * cols
    spread = (iota((cells, rows), 0) // cols == iota((cells, rows), 1)).astype(BF16)
    wide = dot(spread, mask.astype(F32).astype(BF16))
    own = iota((cells, cols), 0) % cols == iota((cells, cols), 1)
    return jnp.sum(jnp.where(own, wide, 0.0), axis=1, keepdims=True)


def start_body(
    block_count,
    owners_in,
    blocks_in,
    counts,
    sea_in,
    tok_in,
    mask_in,
    projector_in,
    overlay_in,
    encoder_in,
    gain_in,
    lookup_in,
    lat_a,
    lat_b,
    to_core,
    to_chip,
    given,
    wanted,
    encoder,
    gain,
    tok,
    sea,
    lookup,
    mask,
    owners,
    blocks,
    projector,
    overlay,
    sems,
):
    lat_even = lax.rem(lax.axis_index("lat"), 2) == 0
    rows, cols, width = tok_in.shape
    sea_rows, _, channels = sea_in.shape
    tok_low = jnp.where(lat_even, rows - SHIFT, 0)
    tok_high = jnp.where(lat_even, 0, rows - SHIFT)
    sea_low = jnp.where(lat_even, sea_rows - HALF, 0)
    sea_high = jnp.where(lat_even, 0, sea_rows - HALF)
    moves = (
        (sea_in, sea),
        (projector_in, projector),
        (mask_in, mask),
        (overlay_in, overlay),
        (owners_in, owners),
        (blocks_in, blocks),
        (encoder_in, encoder),
        (gain_in, gain),
        (tok_in, tok),
        (lookup_in, lookup),
    )
    copies = {}
    for n, (source, target) in enumerate(moves):
        copy = pltpu.make_async_copy(source, target, sems.at[n])
        copy.start()
        copies[id(target)] = copy

    def ready(*targets):
        for target in targets:
            copies.pop(id(target)).wait()

    slot_count = overlay.shape[0] // BLK
    fields = projector.shape[0]
    patches = block_count * BLK
    shape = (slot_count * BLK, 3 * patches)
    ready(owners, blocks)
    places = iota((shape[0], 1), 0)
    target = slot_targets(owners, blocks, counts, places, slot_count, block_count)
    route = (iota(shape, 1) == target).astype(F32).astype(BF16)
    wanted[...] = slot_targets(
        owners, blocks, counts, iota(wanted.shape, 1), slot_count, block_count
    )
    ready(mask, projector, sea)
    parts = jnp.concatenate(split3(projector[...]), axis=0).astype(BF16)
    spread = dot(parts, sea[...].reshape(-1, channels), ((1,), (1,)))
    values = spread[:fields] + spread[fields : 2 * fields] + spread[2 * fields :]
    values = (values * mask_row(mask[...])).astype(BF16)
    put_columns(to_core, to_chip, 0, sea[...], HALF, slice(width, width + channels))
    ready(overlay, tok)
    contrib = dot(values, overlay[...], ((1,), (1,)))
    stacked = jnp.concatenate(split3(contrib), axis=0).astype(BF16)
    routed = dot(stacked, route)
    routed = routed[:fields] + routed[fields : 2 * fields] + routed[2 * fields :]
    count = SHIFT * cols
    lat_a[:count, :width] = tok[pl.ds(tok_low, SHIFT)].reshape(count, width)
    lat_b[:count, :width] = tok[pl.ds(tok_high, SHIFT)].reshape(count, width)
    lat_a[:count, width:] = sea[pl.ds(sea_low, HALF)].reshape(count, channels)
    lat_b[:count, width:] = sea[pl.ds(sea_high, HALF)].reshape(count, channels)
    put_columns(to_core, to_chip, 0, tok[...], SHIFT, slice(0, width))
    parts = [routed[:, k * patches : (k + 1) * patches] for k in range(3)]
    low, high = [], []
    for n in range(2):
        for k in range(3):
            piece = split2(parts[k])[n]
            low.append(piece[:, patches - 128 :])
            high.append(piece[:, :128])
    given[...] = jnp.concatenate(parts, axis=0)
    blank = jnp.zeros((8 - fields, 6 * 128), F32)
    low = jnp.concatenate([jnp.concatenate(low, axis=1), blank], axis=0)
    high = jnp.concatenate([jnp.concatenate(high, axis=1), blank], axis=0)
    lat_a[count:] = jnp.where(lat_even, low, high).astype(BF16)
    lat_b[count:] = jnp.where(lat_even, high, low).astype(BF16)
    ready(encoder, gain, lookup)


def prepare_body(tok, from_a, from_b, side_core, side_chip, grid):
    lat_even = lax.rem(lax.axis_index("lat"), 2) == 0
    lon_even = lax.rem(lax.axis_index("lon"), 2) == 0
    rows, cols, width = tok.shape
    count = SHIFT * cols
    inner = slice(SHIFT, SHIFT + cols)
    north, south = pick(lat_even, from_b[:count, :width], from_a[:count, :width])
    grid[SHIFT : SHIFT + rows, inner] = tok[...].astype(F32)
    grid[:SHIFT, inner] = north.astype(F32).reshape(SHIFT, cols, width)
    grid[SHIFT + rows :, inner] = south.astype(F32).reshape(SHIFT, cols, width)
    west, east = pick(lon_even, side_chip[:, :, :width], side_core[:, :, :width])
    blank = jnp.zeros((SHIFT, SHIFT, width), F32)
    for where, side in ((slice(0, SHIFT), west), (slice(SHIFT + cols, None), east)):
        grid[SHIFT : SHIFT + rows, where] = side.astype(F32)
        grid[:SHIFT, where] = blank
        grid[SHIFT + rows :, where] = blank


def attention_body(
    state,
    near_core,
    near_chip,
    far_one,
    far_two,
    sides,
    gain,
    weight,
    weight_bias,
    pos_bias,
    out_weight,
    projector,
    encoder,
    atm,
    flux,
    grid,
    fields_grid,
    corner,
    key_mask,
    value_mask,
    mixed_rows,
    normed_rows,
    query_rows,
    value_rows,
    key_columns,
):
    rows, cols, width = atm.shape
    padded_rows, padded_cols = rows + 2 * SHIFT, cols + 2 * SHIFT
    band_count, per_band = padded_rows // WIN, padded_cols // WIN
    lat, lat_size = lax.axis_index("lat"), lax.axis_size("lat")
    lat_even = lax.rem(lat, 2) == 0
    lon_even = lax.rem(lax.axis_index("lon"), 2) == 0
    head = width // HEADS
    group = 128 // head
    places = WIN * WIN
    inner = slice(SHIFT, SHIFT + cols)

    def heads_match(shape, first, second):
        match = iota(shape, 0) // first == iota(shape, 1) // second
        return match.astype(F32).astype(BF16)

    key_mask[...] = heads_match(key_mask.shape, head, places)
    value_mask[...] = heads_match(value_mask.shape, places, head)

    fields = encoder.shape[0]
    lon = lax.axis_index("lon")
    span = sides.shape[1]

    def joined(ref, at, step):
        return ref[at, :, :span].astype(F32) + ref[at + step, :, :span].astype(F32)

    at = 2 * SHIFT
    west_side, east_side = pick(lon_even, joined(near_chip, at, 2), joined(near_core, at, 2))
    west_own, east_own = pick(lon_even, joined(near_chip, at + 1, 2), joined(near_core, at + 1, 2))
    lower = lax.rem(lon, 4) < 2
    far_west, far_east = pick(lower, joined(far_two, 0, 1), joined(far_one, 0, 1))
    to_west, own, to_east = [sides[k * fields : (k + 1) * fields] for k in range(3)]
    values = jnp.concatenate(
        [
            own + west_side + east_side,
            far_west + west_own + to_west,
            to_east + east_own + far_east,
            jnp.zeros_like(own),
        ],
        axis=0,
    )
    high, low = split2(values)
    turned = jnp.transpose(jnp.concatenate([high, low, high], axis=0))
    lanes = turned.shape[1]
    kind = (iota((1, 1, lanes), 2) % 16) // 4

    def put_fields(at, start, count):
        part = turned[start : start + count * cols].reshape(count, cols, lanes)
        fields_grid[at : at + count, inner, :lanes] = jnp.where(kind == 0, part, 0.0)
        fields_grid[at : at + count, :SHIFT, :lanes] = jnp.where(
            kind == 1, part[:, cols - SHIFT :], 0.0
        )
        fields_grid[at : at + count, SHIFT + cols :, :lanes] = jnp.where(
            kind == 2, part[:, :SHIFT], 0.0
        )

    put_fields(0, 128 - SHIFT * cols, SHIFT)
    put_fields(SHIFT, 128, rows)
    put_fields(SHIFT + rows, 128 + rows * cols, SHIFT)

    def corners(west, east):
        corner[...] = jnp.zeros(corner.shape, F32)
        last = band_count - 1
        corner[0, 0, :SHIFT, :SHIFT] = west[:SHIFT, :, :width].astype(F32)
        corner[0, 1, :SHIFT, WIN - SHIFT :] = east[:SHIFT, :, :width].astype(F32)
        corner[last, 0, WIN - SHIFT :, :SHIFT] = west[SHIFT : 2 * SHIFT, :, :width].astype(F32)
        corner[last, 1, WIN - SHIFT :, WIN - SHIFT :] = east[
            SHIFT : 2 * SHIFT, :, :width
        ].astype(F32)

    @pl.when(lon_even)
    def _():
        corners(near_chip, near_core)

    @pl.when(jnp.logical_not(lon_even))
    def _():
        corners(near_core, near_chip)

    enc = encoder[...]
    enc = jnp.concatenate([enc, enc, enc, jnp.zeros_like(enc)], axis=0)
    enc_high, enc_low = split2(enc)
    enc_stack = jnp.concatenate([enc_high, enc_high, enc_low], axis=0).astype(BF16)
    span = enc_stack.shape[0]
    lane = iota((places, 2 * places), 1) % places
    crosses = (lane // (places // 2)) != (iota((places, 2 * places), 0) // (places // 2))
    lane128 = iota((places, 2 * places), 1)
    band_rows = per_band * places

    def normalise(b, carry):
        at = pl.multiple_of(b * WIN, WIN)

        fields_here = [
            fields_grid[pl.ds(at, WIN), w * WIN : (w + 1) * WIN, :span].reshape(places, span)
            for w in range(per_band)
        ]
        added = dot(jnp.concatenate(fields_here, axis=0).astype(BF16), enc_stack)
        held = [
            state[pl.ds(at, WIN), w * WIN : (w + 1) * WIN].reshape(places, width)
            for w in range(per_band)
        ]
        held[0] = held[0] + corner[b, 0].reshape(places, width)
        held[-1] = held[-1] + corner[b, 1].reshape(places, width)
        mixed = (jnp.concatenate(held, axis=0) + added).astype(BF16)
        here = pl.ds(pl.multiple_of(b * band_rows, band_rows), band_rows)
        mixed_rows[here] = mixed
        mixed = mixed.astype(F32)
        average = jnp.mean(mixed, axis=-1, keepdims=True)
        centred = mixed - average
        spread = jnp.mean(centred * centred, axis=-1, keepdims=True)
        normed_rows[here] = (centred * lax.rsqrt(spread + 1e-05) * gain[...]).astype(BF16)
        return carry

    lax.fori_loop(0, band_count, normalise, 0, unroll=True)

    left = iota((256, 2 * places), 1) < places
    keys_first = [(at + width) % (3 * width) for at in range(0, 3 * width, 256)]
    for at in keys_first:
        lanes = slice(at, at + 256)
        part = dot(normed_rows[...], weight[:, lanes]) + weight_bias[lanes].reshape(1, 256)
        if at < width:
            query_rows[:, lanes] = (part * head ** (-0.5)).astype(BF16)
        elif at >= 2 * width:
            value_rows[:, at - 2 * width : at - 2 * width + 256] = part.astype(BF16)
        else:
            turned = jnp.transpose(part)
            where = slice(at - width, at - width + 256)
            for n in range(0, band_count * per_band, 2):
                two = turned[:, n * places : (n + 2) * places]
                swapped = pltpu.roll(two, places, 1)
                at_n = 2 * n * places
                key_columns[where, at_n : at_n + 2 * places] = jnp.where(
                    left, two, swapped
                ).astype(BF16)
                at_n += 2 * places
                key_columns[where, at_n : at_n + 2 * places] = jnp.where(
                    left, swapped, two
                ).astype(BF16)

    groups = HEADS // group
    jobs = [(n, g) for n in range(band_count * per_band) for g in range(groups)]
    keys_here, values_here = key_mask[...], value_mask[...]
    first_penalty = jnp.where(lat == 0, -1000000000.0, 0.0)
    last_penalty = jnp.where(lat == lat_size - 1, -1000000000.0, 0.0)
    biases = {}

    def bias_of(n, lanes):
        b = n // per_band
        if (b, lanes.start) not in biases:
            found = pos_bias[:, lanes]
            if b == 0:
                found = found + jnp.where(crosses, first_penalty, 0.0)
            if b == band_count - 1:
                found = found + jnp.where(crosses, last_penalty, 0.0)
            biases[b, lanes.start] = found
        return biases[b, lanes.start]

    def place(job):
        n, g = job
        return slice(n * places, (n + 1) * places), slice(g * group * head, (g + 1) * group * head)

    def scored(job):
        at = job[0] * 2 * places
        part, lanes = place(job)
        k_wide = key_columns[lanes, at : at + 2 * places]
        k_wide = jnp.concatenate([k_wide] * (group // 2), axis=1) * keys_here
        return dot(query_rows[part, lanes], k_wide)

    def weighted(job, scores):
        n, g = job
        weights = []
        for pair in range(group // 2):
            at = pair * 2 * places
            s = scores[:, at : at + 2 * places]
            at += g * group * places
            s = s + bias_of(n, slice(at, at + 2 * places))
            low = jnp.max(jnp.where(lane128 < places, s, -3e38), axis=1, keepdims=True)
            high = jnp.max(jnp.where(lane128 < places, -3e38, s), axis=1, keepdims=True)
            weights.append(jnp.exp(s - jnp.where(lane128 < places, low, high)))
        return jnp.concatenate(weights, axis=1).astype(BF16)

    def summed(job, expo):
        part, lanes = place(job)
        v_wide = jnp.concatenate([value_rows[part, lanes]] * group, axis=0) * values_here
        found = dot(expo, jnp.concatenate([v_wide, values_here], axis=1))
        size = group * head
        normed_rows[part, lanes] = (found[:, :size] / found[:, size:]).astype(BF16)

    scores, expos = {}, {}
    sets = [range(n, n + 2 * groups) for n in range(0, len(jobs), 2 * groups)]
    for t in range(len(sets) + 2):
        for n in sets[t] if t < len(sets) else ():
            scores[n] = scored(jobs[n])
        for n in sets[t - 2] if t >= 2 else ():
            summed(jobs[n], expos.pop(n))
        for n in sets[t - 1] if 0 <= t - 1 < len(sets) else ():
            expos[n] = weighted(jobs[n], scores.pop(n))


    for at in range(0, width, 256):
        lanes = slice(at, at + 256)
        projected = dot(normed_rows[...], out_weight[:, lanes]).astype(BF16).astype(F32)
        result = (mixed_rows[:, lanes].astype(F32) + projected).astype(BF16).astype(F32)
        for n in range(band_count * per_band):
            b, w = divmod(n, per_band)
            grid[b * WIN : (b + 1) * WIN, w * WIN : (w + 1) * WIN, lanes] = result[
                n * places : (n + 1) * places
            ].reshape(WIN, WIN, 256)
    own = grid[SHIFT : SHIFT + rows, inner]
    atm[...] = own.astype(BF16)
    flat = own.reshape(rows * cols, width).astype(BF16)
    flux[...] = dot(projector[...], flat, ((1,), (1,))).astype(BF16)


def conv_body(
    sea, from_a, from_b, side_core, side_chip, near_core, near_chip, kernel, bias, atm, conv, atm_out, grid, shifted, sem
):
    copy = pltpu.make_async_copy(atm, atm_out, sem)
    copy.start()
    lat_even = lax.rem(lax.axis_index("lat"), 2) == 0
    lon_even = lax.rem(lax.axis_index("lon"), 2) == 0
    rows, cols, channels = sea.shape
    width = from_a.shape[1] - channels
    inner = slice(HALF, HALF + cols)
    count = HALF * cols
    north, south = pick(lat_even, from_b[:count, width:], from_a[:count, width:])
    grid[HALF : HALF + rows, inner] = sea[...].astype(F32)
    grid[:HALF, inner] = north.astype(F32).reshape(HALF, cols, channels)
    grid[HALF + rows :, inner] = south.astype(F32).reshape(HALF, cols, channels)

    def lon_halos(west, east, far_west, far_east):
        for where, ref, corner in (
            (slice(0, HALF), west, far_west),
            (slice(HALF + cols, 2 * HALF + cols), east, far_east),
        ):
            grid[HALF : HALF + rows, where] = ref[:, :HALF, width:].astype(F32)
            grid[:HALF, where] = corner[:HALF, :HALF, width:].astype(F32)
            grid[HALF + rows :, where] = corner[SHIFT : SHIFT + HALF, :HALF, width:].astype(F32)

    @pl.when(lon_even)
    def _():
        lon_halos(side_chip, side_core, near_chip, near_core)

    @pl.when(jnp.logical_not(lon_even))
    def _():
        lon_halos(side_core, side_chip, near_core, near_chip)

    padded = grid.shape[1]
    for c in range(0, channels, 128):
        lanes = slice(c, c + 128)
        block = grid[:, :, lanes]
        for v in range(KER):
            turned = pltpu.roll(block, padded - v, 1) if v else block
            shifted[v] = turned[:, :cols]
        for s in range(0, cols, 8):
            total = jnp.broadcast_to(bias[:, lanes].reshape(1, 1, 128), (rows, 8, 128))
            for v in range(KER):
                column = shifted[v, :, s : s + 8]
                for u in range(KER):
                    tap = kernel[u, v : v + 1, lanes].reshape(1, 1, 128)
                    total = total + tap * column[u : u + rows]
            conv[:, s : s + 8, lanes] = total
    copy.wait()


def ocean_body(
    conv,
    flux,
    from_core,
    from_chip,
    route,
    overlay,
    encoder,
    gain,
    expand,
    contract,
    sea,
    wet,
    scale,
    out,
):
    lon_even = lax.rem(lax.axis_index("lon"), 2) == 0
    west, east = pick(lon_even, from_chip[...], from_core[...])
    around = jnp.concatenate([west, flux[...], east], axis=1)
    picked = dot(around, route[...]).astype(BF16)
    forcing = dot(picked, overlay[...])
    high, low = split2(forcing)
    turned = jnp.transpose(jnp.concatenate([high, low, high], axis=0)).astype(BF16)
    enc_high, enc_low = split2(encoder[...])
    enc_stack = jnp.concatenate([enc_high, enc_high, enc_low], axis=0).astype(BF16)
    pre = conv[...] + dot(turned, enc_stack)
    average = jnp.mean(pre, axis=-1, keepdims=True)
    centred = pre - average
    spread = jnp.mean(centred * centred, axis=-1, keepdims=True)
    normed = (centred * lax.rsqrt(spread + 1e-06) * gain[...]).astype(BF16)
    hidden = dot(normed, expand[...])
    hidden = (0.5 * hidden * (1.0 + lax.erf(hidden * 0.5**0.5))).astype(BF16)
    update = dot(hidden, contract[...])
    kept = jnp.concatenate([wet[...]] * (update.shape[1] // 128), axis=1)
    out[...] = (sea[...].astype(F32) + kept * scale[...] * update).astype(BF16)


def tables_body(lookup, wanted, mask, out, route, wet):
    route[...] = (iota(route.shape, 0) == wanted[...]).astype(F32).astype(BF16)
    wet[...] = jnp.broadcast_to(mask_column(mask[...]), wet.shape)
    places = WIN * WIN
    span = 2 * WIN - 1
    width = 256
    entries = lookup.shape[1]
    flip = iota((entries, width), 0) + iota((entries, width), 1) == entries - 1
    parts = jnp.concatenate(split3(lookup[...]), axis=0).astype(BF16)
    parts = dot(parts, flip.astype(F32).astype(BF16))
    turned = parts[:HEADS] + parts[HEADS : 2 * HEADS] + parts[2 * HEADS :]
    middle = (WIN - 1) * (span + 1)
    row = iota((128, 2 * places), 0)
    lane = iota((128, 2 * places), 1) % places
    spread = (row == lane // WIN * span + lane % WIN).astype(F32).astype(BF16)
    spread = jnp.concatenate([spread] * 3, axis=0)
    half = iota((places, 2 * places), 1) < places
    for pair in range(HEADS // 2):
        found = []
        for h in (2 * pair, 2 * pair + 1):
            line = jnp.broadcast_to(turned[h : h + 1], (WIN, width))
            shifted = jnp.concatenate(
                [
                    pltpu.roll(
                        line, (width - middle + span * r) % width, 1, stride=1, stride_axis=0
                    )[:, :128]
                    for r in range(WIN)
                ],
                axis=0,
            )
            parts = jnp.concatenate(split3(shifted), axis=1).astype(BF16)
            found.append(dot(parts, spread))
        out[:, pair * 2 * places : (pair + 1) * 2 * places] = jnp.where(half, *found)


def local(
    atmos_patch_tokens,
    atmos_norm_gain,
    query_key_value_weight,
    query_key_value_bias,
    relative_bias_grid,
    attention_output_weight,
    flux_projector,
    surface_encoder,
    ocean_cell_state,
    land_sea_mask,
    depthwise_conv_kernel,
    depthwise_conv_bias,
    ocean_norm_gain,
    pointwise_expand,
    pointwise_contract,
    layer_update_scale,
    forcing_encoder,
    surface_projector,
    overlay_area_weight,
    owners,
    owner_tile_blocks,
    counts,
):
    lat_size, lon_size = lax.axis_size("lat"), lax.axis_size("lon")
    rows, cols, width = atmos_patch_tokens.shape
    sea_rows, sea_cols, channels = ocean_cell_state.shape
    cells = sea_rows * sea_cols
    patches = rows * cols
    block_count = patches // BLK
    slot_count = owners.shape[2]
    channel_count = flux_projector.shape[1]

    def swaps(pairs):
        return [(a, b) for a, b in pairs] + [(b, a) for a, b in pairs]

    lat_a = swaps([(k, k + 1) for k in range(0, lat_size - 1, 2)])
    lat_b = swaps([(k, k + 1) for k in range(1, lat_size - 1, 2)])
    core = swaps([(k, k + 1) for k in range(0, lon_size, 2)])
    chip = swaps([(k + 1, (k + 2) % lon_size) for k in range(0, lon_size, 2)])
    assert lon_size % 4 == 0
    lower = [k for k in range(lon_size) if k % 4 < 2]
    far_near = swaps([(k, k + 2) for k in lower])
    far_next = swaps([(k, (k - 2) % lon_size) for k in lower])

    tok, sea = atmos_patch_tokens, ocean_cell_state
    overlay = overlay_area_weight.reshape(slot_count * BLK, cells)
    fields = surface_projector.shape[1]
    lat_pack = struct((SHIFT * cols + 8, width + channels), BF16)
    side_pack = struct((rows, SHIFT, width + channels), BF16)
    firsts = (
        owners,
        owner_tile_blocks,
        counts,
        sea,
        tok,
        land_sea_mask,
        surface_projector.T,
        overlay,
        surface_encoder,
        atmos_norm_gain.reshape(1, width),
        relative_bias_grid,
    )

    def like(n):
        return struct(firsts[n].shape, firsts[n].dtype)

    firsts = tuple(
        x if n == 2 else pltpu.with_memory_space_constraint(x, pltpu.HBM)
        for n, x in enumerate(firsts)
    )
    to_a, to_b, to_core, to_chip, given, wanted, encoder, gain, tok, sea, lookup, mask = call(
        functools.partial(start_body, block_count),
        (lat_pack,) * 2
        + (side_pack,) * 2
        + (struct((3 * fields, patches), F32), struct((1, slot_count * BLK), jnp.int32))
        + (like(8), like(9), like(4), like(3), like(10), like(5)),
        firsts,
        specs=[smem() if n == 2 else anywhere() for n in range(len(firsts))],
        scratch=[pltpu.SMEM(x.shape, jnp.int32) for x in firsts[:2]]
        + [pltpu.VMEM(firsts[n].shape, firsts[n].dtype) for n in (6, 7)]
        + [pltpu.SemaphoreType.DMA((10,))],
        flops=3e8,
    )
    from_a = lax.ppermute(to_a, "lat", lat_a)
    from_b = lax.ppermute(to_b, "lat", lat_b)
    side_core = lax.ppermute(to_core, "lon", core)
    side_chip = lax.ppermute(to_chip, "lon", chip)

    near_pack = struct((2 * SHIFT + 4, SHIFT, width + channels), BF16)
    far_pack = struct((2, fields, patches + 256), BF16)
    to_core, to_chip, to_one, to_two, sides = call(
        functools.partial(pack_body, cols, width, sea_cols),
        (near_pack, near_pack, far_pack, far_pack, struct((3 * fields, patches + 256), F32)),
        (from_a, from_b, given),
    )
    near_core = lax.ppermute(to_core, "lon", core)
    near_chip = lax.ppermute(to_chip, "lon", chip)
    far_one = lax.ppermute(to_one, "lon", far_near)
    far_two = lax.ppermute(to_two, "lon", far_next)

    pos_bias, route, wet = call(
        tables_body,
        (
            struct((WIN * WIN, HEADS * WIN * WIN), F32),
            struct((3 * patches, slot_count * BLK), BF16),
            struct((cells, 128), F32),
        ),
        (lookup, wanted, mask),
        flops=5e8,
    )
    padded = (rows + 2 * SHIFT, cols + 2 * SHIFT)
    (state,) = call(
        prepare_body,
        (pltpu.VMEM((*padded, width), F32),),
        (tok, from_a, from_b, side_core, side_chip),
    )
    atm, flux = call(
        attention_body,
        (pltpu.VMEM((rows, cols, width), BF16), struct((channel_count, patches), BF16)),
        (
            state,
            near_core,
            near_chip,
            far_one,
            far_two,
            sides,
            gain,
            query_key_value_weight,
            query_key_value_bias,
            pos_bias,
            attention_output_weight,
            flux_projector.T,
            encoder,
        ),
        scratch=(
            pltpu.VMEM((*padded, width), F32),
            pltpu.VMEM((*padded, 128), F32),
            pltpu.VMEM((padded[0] // WIN, 2, WIN, WIN, width), F32),
            pltpu.VMEM((128, 128 * HEADS // width * WIN * WIN), BF16),
            pltpu.VMEM((128 * HEADS // width * WIN * WIN, 128), BF16),
            pltpu.VMEM((padded[0] * padded[1], width), BF16),
            pltpu.VMEM((padded[0] * padded[1], width), BF16),
            pltpu.VMEM((padded[0] * padded[1], width), BF16),
            pltpu.VMEM((padded[0] * padded[1], width), BF16),
            pltpu.VMEM((width, 2 * padded[0] * padded[1]), BF16),
        ),
        flops=3e9,
    )
    flux_core = lax.ppermute(flux, "lon", core)
    flux_chip = lax.ppermute(flux, "lon", chip)

    conv, atm = call(
        conv_body,
        (struct((sea_rows, sea_cols, channels), F32), struct((rows, cols, width), BF16)),
        (
            sea,
            from_a,
            from_b,
            side_core,
            side_chip,
            near_core,
            near_chip,
            depthwise_conv_kernel,
            depthwise_conv_bias.reshape(1, channels),
            atm,
        ),
        out_specs=[vmem(), anywhere()],
        scratch=(
            pltpu.VMEM((sea_rows + 2 * HALF, sea_cols + 8, channels), F32),
            pltpu.VMEM((KER, sea_rows + 2 * HALF, sea_cols, 128), F32),
            pltpu.SemaphoreType.DMA(()),
        ),
        flops=2e9,
    )
    (ocean,) = call(
        ocean_body,
        (struct((cells, channels), BF16),),
        (
            conv.reshape(cells, channels),
            flux,
            flux_core,
            flux_chip,
            route,
            overlay,
            forcing_encoder,
            ocean_norm_gain.reshape(1, channels),
            pointwise_expand,
            pointwise_contract,
            sea.reshape(cells, channels),
            wet,
            layer_update_scale.reshape(1, channels),
        ),
        flops=1e9,
    )
    return (atm, ocean.reshape(sea_rows, sea_cols, channels))


def solution(mesh):
    grid = P("lat", "lon", None)
    placed = (
        (grid,)
        + (P(),) * 7
        + (grid, P("lat", "lon"))
        + (P(),) * 8
        + (P("lat", "lon", None, None, None), grid, grid, P("lat", "lon"))
    )
    return jax.shard_map(
        local,
        mesh=mesh,
        in_specs=placed,
        out_specs=(grid, grid),
        check_vma=False,
    )
```
